256 devices in a mesh: row: 32 (over y, z_lo, core), col: 8 (over x, z_hi).
Axes of the slice: x: 4, y: 4, z: 8 (z_hi: 2, z_lo: 4; z = z_hi * 4 + z_lo), core: 2. Of those that a mesh axis runs over, the one named last changes fastest.
Arguments:
- object_field: bfloat16 [2, 8192, 8192], P(None, 'row', 'col'), may hold values from -6 to 6
- probe: float32 [2, 2, 256, 256], replicated, may hold values from -5 to 5
- measured: bfloat16 [32, 8, 12, 256, 256], P('row', 'col'), may hold values from 0.3984375 to 4
- positions: int32 [32, 8, 12, 2], P('row', 'col'), may hold values from 0 to 1023, as said below
- counts: int32 [32, 8], P('row', 'col'), may hold values from 1 to 12, as said below
Outputs:
- object_grad: float32 [2, 8192, 8192], P(None, 'row', 'col')
- probe_grad: float32 [2, 2, 256, 256], replicated
The draws below stay inside these ranges and needn't reach their ends.
Inputs may be any that keep to these rules, and one draw needn't show every extreme that they name: positions[i, j, s, 0] lies in 0 to 255 and positions[i, j, s, 1] in 0 to 1023 for every slot, live or not. `counts`: some tile has all 12 slots live.
All inputs are finite; a program needn't handle non-finite values.
Results may differ from the reference program's by a relative error of at most 0.0048.
The reference program's roundings to bfloat16 on the way (of `patch`, `wave` and `weighted`) count: a program that leaves them out, or rounds other values in their place, can miss the bound.
Values may be sent and summed in bfloat16 or wider, within the bound.
No kernel may reach another device: no remote copies, remote signals or barrier semaphores. Data moves between devices by JAX's collectives and lax.ppermute only.
A program may use at most 128 MiB of HBM per device.

```python
import math
import jax
import jax.numpy as jnp
from jax import lax

P_SIZE = 256
MODES = 2
TILE_R = 256
TILE_C = 1024
SLOTS = 12
GRID_R = 32
GRID_C = 8
OBJ_R = 8192
OBJ_C = 8192
N_ROW = 32
N_COL = 8


def draw_positions(key, part):
    key_rows = jax.random.fold_in(key, 11)
    key_cols = jax.random.fold_in(key, 12)
    rows = jax.random.randint(key_rows, (GRID_R, GRID_C, SLOTS, 1), 0, TILE_R)
    cols = jax.random.randint(key_cols, (GRID_R, GRID_C, SLOTS, 1), 0, TILE_C)
    return jnp.concatenate([rows, cols], 3).astype(jnp.int32)


def draw_counts(key, part):
    key_first = jax.random.fold_in(key, 21)
    key_second = jax.random.fold_in(key, 22)
    key_pick = jax.random.fold_in(key, 23)
    first = jax.random.randint(key_first, (GRID_R * GRID_C,), 0, SLOTS)
    second = jax.random.randint(key_second, (GRID_R * GRID_C,), 0, SLOTS)
    counts = 1 + first * second // (SLOTS - 1)
    chosen = jax.random.randint(key_pick, (), 0, GRID_R * GRID_C)
    counts = counts.at[chosen].set(SLOTS)
    return counts.reshape(GRID_R, GRID_C).astype(jnp.int32)


def block_levels(stream_key, shape, cuts, smallest, top_value):
    gain, own = 1.0, jax.random.fold_in(stream_key, 6)
    for position, blocks in cuts:
        steps = jnp.exp(jax.random.uniform(jax.random.fold_in(own, position), (blocks,), jnp.float32, smallest / len(cuts), top_value / len(cuts)))
        gain = gain * jnp.repeat(steps, shape[position] // blocks).reshape([-1 if axis == position else 1 for axis in range(len(shape))])
    return gain


def bell_draw(own_key, shape, deviation, limit, shards=(), held_as=jnp.bfloat16):
    values = jax.random.normal(own_key, shape, jnp.float32) * deviation
    if len(shards) > 0:
        values = block_levels(own_key, shape, shards, -0.22, 0.18) * values
    return jnp.clip(values, min=-limit, max=limit).astype(held_as)


def setup_inputs(seed: int = 0) -> dict:
    keys = jax.random.split(jax.random.key(seed), 6)
    object_field = bell_draw(keys[0], (2, OBJ_R, OBJ_C), 1.0, 6.0, ((1, 32), (2, 8)))
    probe = bell_draw(keys[1], (MODES, 2, P_SIZE, P_SIZE), 0.7, 5.0, (), jnp.float32)
    measured = jnp.clip(jnp.exp(math.log(4.0) - 2.306499 * jax.random.uniform(keys[2], (GRID_R, GRID_C, SLOTS, P_SIZE, P_SIZE), jnp.float32) ** block_levels(keys[2], (GRID_R, GRID_C, SLOTS, P_SIZE, P_SIZE), ((0, 32), (1, 8)), -0.2, 0.2)), 0.3984375, 4.0).astype(jnp.bfloat16)
    positions = draw_positions(jax.random.fold_in(keys[5], 71), 0)
    counts = draw_counts(jax.random.fold_in(keys[5], 71), 0)
    return dict(object_field=object_field, probe=probe, measured=measured, positions=positions, counts=counts)


def dft_tables(size, sign):
    index = jnp.arange(size, dtype=jnp.int32)
    phase = index[:, None] * index[None, :] % size
    angle = 2.0 * jnp.pi / size * phase.astype(jnp.float32)
    cosine = jnp.cos(angle) / jnp.sqrt(jnp.float32(size))
    sine = sign * jnp.sin(angle) / jnp.sqrt(jnp.float32(size))
    left = jnp.stack([jnp.stack([cosine, sine], 0), jnp.stack([-sine, cosine], 0)], 0)
    right = jnp.stack([jnp.stack([cosine, -sine], 1), jnp.stack([sine, cosine], 1)], 0)
    return (left.astype(jnp.bfloat16), right.astype(jnp.bfloat16))

def transform(field, left, right):
    half = jnp.einsum('ocij,mcjk->moik', left.astype(jnp.float32), field.astype(jnp.float32), precision=lax.Precision.HIGHEST)
    half = half.astype(jnp.bfloat16)
    return jnp.einsum('mcij,cjdk->mdik', half.astype(jnp.float32), right.astype(jnp.float32), precision=lax.Precision.HIGHEST)

def position_terms(patch, frame, probe, tables):
    fwd_left, fwd_right, inv_left, inv_right = tables
    obj = patch.astype(jnp.float32)
    obj_re, obj_im = (obj[0], obj[1])
    pro_re, pro_im = (probe[:, 0], probe[:, 1])
    wave = jnp.stack([pro_re * obj_re - pro_im * obj_im, pro_re * obj_im + pro_im * obj_re], 1).astype(jnp.bfloat16)
    spectrum = transform(wave, fwd_left, fwd_right)
    intensity = lax.optimization_barrier(jnp.sum(spectrum * spectrum, axis=(0, 1)))
    amplitude = jnp.sqrt(intensity + 1.0)
    factor = 1.0 - frame.astype(jnp.float32) / amplitude
    weighted = (spectrum * factor).astype(jnp.bfloat16)
    back = transform(weighted, inv_left, inv_right)
    back_re, back_im = (back[:, 0], back[:, 1])
    obj_grad = jnp.stack([lax.optimization_barrier(jnp.sum(pro_re * back_re + pro_im * back_im, 0)), lax.optimization_barrier(jnp.sum(pro_re * back_im - pro_im * back_re, 0))], 0)
    probe_part = jnp.stack([obj_re * back_re + obj_im * back_im, obj_re * back_im - obj_im * back_re], 1)
    return (obj_grad, probe_part)

def reference(object_field, probe, measured, positions, counts):
    fwd_left, fwd_right = dft_tables(P_SIZE, 1.0)
    inv_left, inv_right = dft_tables(P_SIZE, -1.0)
    tables = (fwd_left, fwd_right, inv_left, inv_right)
    padded = jnp.pad(object_field, ((0, 0), (0, P_SIZE), (0, P_SIZE)))
    grad = jnp.zeros(padded.shape, jnp.float32)
    probe_sum = jnp.zeros(probe.shape, jnp.float32)
    total = N_ROW * N_COL * SLOTS
    items = jnp.arange(total, dtype=jnp.int32)
    tile_r = items // (N_COL * SLOTS)
    tile_c = items // SLOTS % N_COL
    slot = items % SLOTS
    flat_pos = positions.reshape(total, 2).astype(jnp.int32)
    flat_counts = counts.reshape(N_ROW * N_COL).astype(jnp.int32)
    live = slot < flat_counts[items // SLOTS]
    start_r = (tile_r * TILE_R + flat_pos[:, 0]).astype(jnp.int32)
    start_c = (tile_c * TILE_C + flat_pos[:, 1]).astype(jnp.int32)
    flat_measured = measured.reshape(total, P_SIZE, P_SIZE)
    zero = jnp.zeros((), jnp.int32)

    def step(carry, item):
        index, row_at, col_at, alive = item

        def active(state):
            grad_now, probe_now = state
            patch = lax.dynamic_slice(padded, (zero, row_at, col_at), (2, P_SIZE, P_SIZE))
            obj_grad, probe_part = position_terms(patch, flat_measured[index], probe, tables)
            old = lax.dynamic_slice(grad_now, (zero, row_at, col_at), (2, P_SIZE, P_SIZE))
            grad_now = lax.dynamic_update_slice(grad_now, old + obj_grad, (zero, row_at, col_at))
            return (grad_now, probe_now + probe_part)
        return (lax.cond(alive, active, lambda state: state, carry), None)
    (grad, probe_sum), _ = lax.scan(step, (grad, probe_sum), (items, start_r, start_c, live))
    object_grad = grad[:, :TILE_R * N_ROW, :TILE_C * N_COL]
    probe_grad = probe_sum / jnp.sqrt(jnp.float32(total))
    return (object_grad, probe_grad)
```

```python
import math

import jax
import jax.numpy as jnp
import numpy as np
from jax import lax
from jax.experimental import pallas as pl
from jax.experimental.pallas import tpu as pltpu
from jax.sharding import PartitionSpec as P

f32 = jnp.float32
bf16 = jnp.bfloat16


def shifted(x, axis, by):
    peers = lax.axis_size(axis)
    pairs = [(i, i + by) for i in range(peers) if 0 <= i + by < peers]
    return lax.ppermute(x, axis, pairs)


FIELDS = {
    "core": ("row", 0, 1),
    "zlo": ("row", 1, 2),
    "y": ("row", 3, 2),
    "row_hi": ("row", 1, 4),
    "zhi": ("col", 0, 1),
    "x": ("col", 1, 2),
    "col": ("col", 0, 3),
}


def partner(v, field, d):
    axis, low, _ = FIELDS[field]
    return lax.ppermute(v, axis, [(i, i ^ (d << low)) for i in range(lax.axis_size(axis))])


def place(field):
    axis, low, bits = FIELDS[field]
    return (lax.axis_index(axis) >> low) & ((1 << bits) - 1)


def scatter_sum(v, field, dtype):
    n = 1 << FIELDS[field][2]
    g = place(field)
    k = v.shape[0] // n
    total = lax.dynamic_slice_in_dim(v, g * k, k, 0)
    got = [
        partner(lax.dynamic_slice_in_dim(v, (g ^ d) * k, k, 0).astype(dtype), field, d)
        for d in range(1, n)
    ]
    for part in got:
        total = total + part.astype(f32)
    return total


def full_sum(v, field, dtype):
    n = 1 << FIELDS[field][2]
    sent = v.astype(dtype)
    parts = [sent.astype(f32)] + [partner(sent, field, d).astype(f32) for d in range(1, n)]
    while len(parts) > 1:
        parts = [parts[i] + parts[i + 1] for i in range(0, len(parts), 2)]
    return parts[0]


def gather(v, field, dtype):
    n = 1 << FIELDS[field][2]
    g = place(field)
    k = v.shape[0]
    sent = v.astype(dtype)
    got = [partner(sent, field, d) for d in range(1, n)]
    out = jnp.zeros((n * k,) + v.shape[1:], dtype)
    out = lax.dynamic_update_slice_in_dim(out, sent, g * k, 0)
    for d in range(1, n):
        out = lax.dynamic_update_slice_in_dim(out, got[d - 1], (g ^ d) * k, 0)
    return out


PLAN = (
    (scatter_sum, "core", bf16),
    (scatter_sum, "zlo", bf16),
    (full_sum, "y", f32),
    (full_sum, "x", f32),
    (full_sum, "zhi", f32),
    (gather, "zlo", bf16),
    (gather, "core", bf16),
)


def reduce_all(v):
    for step, field, dtype in PLAN:
        v = step(v, field, dtype)
    return v.astype(f32)


def dft_parts(size):
    index = np.arange(size)
    phase = (index[:, None] * index[None, :]) % size
    angle = 2.0 * np.pi / size * phase
    cosine = (np.cos(angle) / np.sqrt(size)).astype(jnp.bfloat16).astype(np.float32)
    sine = (np.sin(angle) / np.sqrt(size)).astype(jnp.bfloat16).astype(np.float32)
    return cosine, sine


def tables(size):
    half = size // 2
    c, s = dft_parts(size)
    order = np.concatenate([np.arange(0, size, 2), np.arange(1, size, 2)])
    fc, fs = c[order], s[order]
    left = np.block([[fc, fs], [-fs, fc]])
    cols = []
    for q in range(2):
        pick = order[q * half : (q + 1) * half]
        cols.append(np.block([[c[:, pick], -s[:, pick]], [s[:, pick], c[:, pick]]]))
    right = np.concatenate(cols, 1)
    gl, gr = [], []
    for q in range(2):
        ce, se = c[:half, q::2], s[:half, q::2]
        gl.append(np.block([[ce, -se], [se, ce]]))
        cr, sr = c[q::2, :half], s[q::2, :half]
        gr.append(np.block([[cr, sr], [-sr, cr]]))
    perm = np.zeros((size, size), np.float32)
    perm[np.arange(size), order] = 1.0
    to = lambda a: jnp.asarray(np.asarray(a, np.float32).astype(jnp.bfloat16))
    return to(left), to(right), to(np.stack(gl)), to(np.stack(gr)), to(perm), to(perm.T)


def prep_kernel(frames, rows, cols, out):
    def one(s, _):
        a = jnp.dot(rows[...], frames[s], preferred_element_type=f32).astype(bf16)
        out[s] = jnp.dot(a, cols[...], preferred_element_type=f32).astype(bf16)
        return 0

    lax.fori_loop(0, frames.shape[0], one, 0)


def main_kernel(
    scale, pos, cnt, own, below, strip, corner, probe, frames, left, right, gl, gr,
    g_own, g_below, g_strip, g_corner, p_out,
    ext, gext, pat, xs, hs, ws, hb, bk,
):
    n = 256
    h = 128
    tr, tc = own.shape[1], own.shape[2]
    ch = 16
    for p in range(2):
        for src, r0, c0 in ((own, 0, 0), (below, tr, 0), (strip, 0, tc), (corner, tr, tc)):
            for b in range(src.shape[2] // 128):
                ext[p, c0 // 128 + b, r0 : r0 + src.shape[1], :] = src[p, :, b * 128 : (b + 1) * 128].astype(f32)
    gext[...] = jnp.zeros_like(gext)
    p_out[...] = jnp.zeros_like(p_out)

    def step(s, _):
        r = pos[s, 0]
        c = pos[s, 1]
        cb = c // 128
        sh = c - cb * 128
        back_sh = lax.rem(384 - sh, 384)
        for i in range(0, n, ch):
            o = []
            for p in range(2):
                w = jnp.concatenate([ext[p, cb + b, pl.ds(r + i, ch), :] for b in range(3)], 1)
                w = pltpu.roll(w, back_sh, 1)[:, :n]
                pat[p, i : i + ch, :] = w
                o.append(w)
            for m in range(2):
                pr = probe[m, 0, i : i + ch, :]
                pi = probe[m, 1, i : i + ch, :]
                xs[i : i + ch, m * n : (m + 1) * n] = (pr * o[0] - pi * o[1]).astype(bf16)
                xs[n + i : n + i + ch, m * n : (m + 1) * n] = (pr * o[1] + pi * o[0]).astype(bf16)
        for m in range(2):
            half = jnp.dot(left[...], xs[:, m * n : (m + 1) * n], preferred_element_type=f32)
            hs[m * n : (m + 1) * n, 0:n] = half[0:n].astype(bf16)
            hs[m * n : (m + 1) * n, n : 2 * n] = half[n : 2 * n].astype(bf16)
        s0 = jnp.dot(hs[0:n, :], right[...], preferred_element_type=f32)
        s1 = jnp.dot(hs[n : 2 * n, :], right[...], preferred_element_type=f32)
        for i in range(0, n, ch):
            rows = i % h
            par = i // h
            for q in range(2):
                t = [v[i : i + ch, q * n : (q + 1) * n] for v in (s0, s1)]
                e = t[0] * t[0] + t[1] * t[1]
                inten = e[:, :h] + e[:, h:] + 1.0
                f = 1.0 - frames[s, i : i + ch, q * h : (q + 1) * h].astype(f32) * lax.rsqrt(inten)
                for m in range(2):
                    for part in range(2):
                        ws[par, part * h + rows : part * h + rows + ch, m * n + q * h : m * n + (q + 1) * h] = (
                            t[m][:, part * h : (part + 1) * h] * f
                        ).astype(bf16)
        for m in range(2):
            e = jnp.dot(gl[0], ws[0, :, m * n : (m + 1) * n], preferred_element_type=f32)
            d = jnp.dot(gl[1], ws[1, :, m * n : (m + 1) * n], preferred_element_type=f32)
            for i in range(0, h, ch):
                for part in range(2):
                    a = e[part * h + i : part * h + i + ch]
                    b = d[part * h + i : part * h + i + ch]
                    up = (a + b).astype(bf16)
                    dn = (a - b).astype(bf16)
                    for q in range(2):
                        hb[q, m * n + i : m * n + i + ch, part * h : (part + 1) * h] = up[:, q * h : (q + 1) * h]
                        hb[q, m * n + h + i : m * n + h + i + ch, part * h : (part + 1) * h] = dn[:, q * h : (q + 1) * h]
        e = [jnp.dot(hb[0, m * n : (m + 1) * n, :], gr[0], preferred_element_type=f32) for m in range(2)]
        d = [jnp.dot(hb[1, m * n : (m + 1) * n, :], gr[1], preferred_element_type=f32) for m in range(2)]
        zero = jnp.zeros((ch, 128), f32)
        for i in range(0, n, ch):
            ore = pat[0, i : i + ch, :]
            oim = pat[1, i : i + ch, :]
            acc_re = acc_im = None
            for m in range(2):
                a = e[m][i : i + ch]
                b = d[m][i : i + ch]
                up = a + b
                dn = a - b
                bre = jnp.concatenate([up[:, :h], dn[:, :h]], 1)
                bim = jnp.concatenate([up[:, h:], dn[:, h:]], 1)
                pr = probe[m, 0, i : i + ch, :]
                pi = probe[m, 1, i : i + ch, :]
                gre = pr * bre + pi * bim
                gim = pr * bim - pi * bre
                acc_re = gre if m == 0 else acc_re + gre
                acc_im = gim if m == 0 else acc_im + gim
                p_out[m, 0, i : i + ch, :] += ore * bre + oim * bim
                p_out[m, 1, i : i + ch, :] += ore * bim - oim * bre
            for p, v in ((0, acc_re), (1, acc_im)):
                v = pltpu.roll(jnp.concatenate([v, zero], 1), sh, 1)
                for b in range(3):
                    gext[p, cb + b, pl.ds(r + i, ch), :] += v[:, b * 128 : (b + 1) * 128]
        return 0

    lax.fori_loop(0, cnt[0], step, 0)
    p_out[...] = p_out[...] * scale
    for p in range(2):
        for dst, r0, c0 in ((g_own, 0, 0), (g_below, tr, 0), (g_strip, 0, tc), (g_corner, tr, tc)):
            for b in range(dst.shape[2] // 128):
                dst[p, :, b * 128 : (b + 1) * 128] = gext[p, c0 // 128 + b, r0 : r0 + dst.shape[1], :].astype(dst.dtype)


def body(object_field, probe, measured, positions, counts):
    size = probe.shape[-1]
    tile_rows, tile_cols = object_field.shape[1:]
    slots = measured.shape[2]
    left, right, gl, gr, perm, perm_t = tables(size)
    vmem = pl.BlockSpec(memory_space=pltpu.VMEM)
    smem = pl.BlockSpec(memory_space=pltpu.SMEM)

    strip = shifted(object_field[:, :, :size], "col", -1)
    below = shifted(object_field, "row", -1)
    corner = shifted(strip, "row", -1)
    frames = pl.pallas_call(
        prep_kernel,
        out_shape=jax.ShapeDtypeStruct(measured.shape[2:], bf16),
        in_specs=[vmem] * 3,
        out_specs=vmem,
        cost_estimate=pl.CostEstimate(flops=slots * 4 * size**3, bytes_accessed=4 * slots * size * size, transcendentals=0),
    )(measured[0, 0], perm, perm_t)

    total = slots * lax.axis_size("row") * lax.axis_size("col")
    scale = 1.0 / math.sqrt(total)
    rows, cols = tile_rows + size, tile_cols + size
    g_own, g_below, g_strip, g_corner, p_sum = pl.pallas_call(
        lambda *refs: main_kernel(scale, *refs),
        out_shape=(
            jax.ShapeDtypeStruct((2, tile_rows, tile_cols), f32),
            jax.ShapeDtypeStruct((2, size, tile_cols), bf16),
            jax.ShapeDtypeStruct((2, tile_rows, size), bf16),
            jax.ShapeDtypeStruct((2, size, size), bf16),
            jax.ShapeDtypeStruct(probe.shape, f32),
        ),
        in_specs=[smem, smem] + [vmem] * 10,
        out_specs=[vmem] * 5,
        scratch_shapes=[
            pltpu.VMEM((2, cols // 128, rows, 128), f32),
            pltpu.VMEM((2, cols // 128, rows, 128), f32),
            pltpu.VMEM((2, size, size), f32),
            pltpu.VMEM((2 * size, 2 * size), bf16),
            pltpu.VMEM((2 * size, 2 * size), bf16),
            pltpu.VMEM((2, size, 2 * size), bf16),
            pltpu.VMEM((2, 2 * size, size), bf16),
            pltpu.VMEM((8, 128), f32),
        ],
        cost_estimate=pl.CostEstimate(flops=slots * 2**30, bytes_accessed=16 * 2**20, transcendentals=0),
    )(positions[0, 0], counts[0], object_field, below, strip, corner, probe, frames, left, right, gl, gr)

    from_above = shifted(g_corner, "row", 1)
    side = shifted((g_strip.astype(f32) + from_above.astype(f32)).astype(bf16), "col", 1)
    band = shifted(g_below, "row", 1)
    probe_grad = reduce_all(p_sum.reshape(-1, size)).reshape(probe.shape)
    object_grad = g_own + band.astype(f32)
    object_grad = object_grad.at[:, :, :size].add(side.astype(f32))
    return (object_grad, probe_grad)


def solution(mesh):
    placed = (
        P(None, "row", "col"),
        P(),
        P("row", "col", None, None, None),
        P("row", "col", None, None),
        P("row", "col"),
    )
    return jax.shard_map(
        body, mesh=mesh, in_specs=placed, out_specs=(P(None, "row", "col"), P()), check_vma=False
    )
```

```python
import math

import jax
import jax.numpy as jnp
import numpy as np
from jax import lax
from jax.experimental import pallas as pl
from jax.experimental.pallas import tpu as pltpu
from jax.sharding import PartitionSpec as P


f32 = jnp.float32
bf16 = jnp.bfloat16


def shifted(x, axis, by):
    peers = lax.axis_size(axis)
    pairs = [(i, i + by) for i in range(peers) if 0 <= i + by < peers]
    return lax.ppermute(x, axis, pairs)


FIELDS = {
    "core": ("row", 0, 1),
    "zlo": ("row", 1, 2),
    "y": ("row", 3, 2),
    "row_hi": ("row", 1, 4),
    "zhi": ("col", 0, 1),
    "x": ("col", 1, 2),
    "col": ("col", 0, 3),
}


def partner(v, field, d):
    axis, low, _ = FIELDS[field]
    return lax.ppermute(v, axis, [(i, i ^ (d << low)) for i in range(lax.axis_size(axis))])


def place(field):
    axis, low, bits = FIELDS[field]
    return (lax.axis_index(axis) >> low) & ((1 << bits) - 1)


def scatter_sum(v, field, dtype):
    n = 1 << FIELDS[field][2]
    g = place(field)
    k = v.shape[0] // n
    total = lax.dynamic_slice_in_dim(v, g * k, k, 0)
    got = [
        partner(lax.dynamic_slice_in_dim(v, (g ^ d) * k, k, 0).astype(dtype), field, d)
        for d in range(1, n)
    ]
    for part in got:
        total = total + part.astype(f32)
    return total


def full_sum(v, field, dtype):
    n = 1 << FIELDS[field][2]
    sent = v.astype(dtype)
    parts = [sent.astype(f32)] + [partner(sent, field, d).astype(f32) for d in range(1, n)]
    while len(parts) > 1:
        parts = [parts[i] + parts[i + 1] for i in range(0, len(parts), 2)]
    return parts[0]


def gather(v, field, dtype):
    n = 1 << FIELDS[field][2]
    g = place(field)
    k = v.shape[0]
    sent = v.astype(dtype)
    got = [partner(sent, field, d) for d in range(1, n)]
    out = jnp.zeros((n * k,) + v.shape[1:], dtype)
    out = lax.dynamic_update_slice_in_dim(out, sent, g * k, 0)
    for d in range(1, n):
        out = lax.dynamic_update_slice_in_dim(out, got[d - 1], (g ^ d) * k, 0)
    return out


PLAN = (
    (scatter_sum, "core", bf16),
    (scatter_sum, "y", bf16),
    (full_sum, "x", bf16),
    (full_sum, "zlo", bf16),
    (full_sum, "zhi", bf16),
    (gather, "y", bf16),
    (gather, "core", bf16),
)


def reduce_all(v):
    for step, field, dtype in PLAN:
        v = step(v, field, dtype)
    return v.astype(f32)


def dft_parts(size):
    index = np.arange(size)
    phase = (index[:, None] * index[None, :]) % size
    angle = 2.0 * np.pi / size * phase
    cosine = (np.cos(angle) / np.sqrt(size)).astype(jnp.bfloat16).astype(np.float32)
    sine = (np.sin(angle) / np.sqrt(size)).astype(jnp.bfloat16).astype(np.float32)
    return cosine, sine


def tables(size):
    half = size // 2
    c, s = dft_parts(size)
    order = np.concatenate([np.arange(0, size, 2), np.arange(1, size, 2)])
    fc, fs = c[order], s[order]
    left = np.block([[fc, fs], [-fs, fc]])
    cols = []
    for q in range(2):
        pick = order[q * half : (q + 1) * half]
        cols.append(np.block([[c[:, pick], -s[:, pick]], [s[:, pick], c[:, pick]]]))
    right = np.concatenate(cols, 1)
    gl, gr = [], []
    for q in range(2):
        ce, se = c[:half, q::2], s[:half, q::2]
        gl.append(np.block([[ce, -se], [se, ce]]))
        cr, sr = c[q::2, :half], s[q::2, :half]
        gr.append(np.block([[cr, sr], [-sr, cr]]))
    perm = np.zeros((size, size), np.float32)
    perm[np.arange(size), order] = 1.0
    to = lambda a: jnp.asarray(np.asarray(a, np.float32).astype(jnp.bfloat16))
    return to(left), to(right), to(np.stack(gl)), to(np.stack(gr)), to(perm), to(perm.T)


def prep_kernel(frames, rows, cols, out):
    def one(s, _):
        a = jnp.dot(rows[...], frames[s], preferred_element_type=f32).astype(bf16)
        out[s] = jnp.dot(a, cols[...], preferred_element_type=f32).astype(bf16)
        return 0

    lax.fori_loop(0, frames.shape[0], one, 0)


def positions_pass(
    pos, cnt, wanted, base, blocks, clear, probe, frames, tables, p_out,
    ext, gext, xs, hs, sp, ws, ib, hb, eb, todo,
):
    left, right, gl, gr = tables
    n = probe.shape[-1]
    h = n // 2
    ch = 16
    todo[0] = 0

    def pick(s, k):
        take = wanted(pos[s, 1])

        @pl.when(take)
        def _():
            todo[k] = s

        return k + take.astype(jnp.int32)

    count = lax.fori_loop(0, cnt[0], pick, 0)
    last = jnp.maximum(count - 1, 0)

    def window(t):
        s = todo[jnp.clip(t, 0, last)]
        c = pos[s, 1]
        sh = lax.rem(c, 128)
        cb = jnp.clip(c // 128 - base, 0, blocks - 3)
        return s, pos[s, 0], cb, sh, lax.rem(384 - sh, 384)

    def patch_rows(win, i, ch=16):
        _, r, cb, _, unshift = win
        out = []
        for p in range(2):
            w = jnp.concatenate([ext[p, cb + b, pl.ds(r + i, ch), :] for b in range(3)], 1)
            out.append(pltpu.roll(w, unshift, 1)[:, :n])
        return out

    def wave_rows(win, i):
        o = patch_rows(win, i)
        for m in range(2):
            pr = probe[m, 0, i : i + ch, :]
            pi = probe[m, 1, i : i + ch, :]
            xs[m, i : i + ch, :] = (pr * o[0] - pi * o[1]).astype(bf16)
            xs[m, n + i : n + i + ch, :] = (pr * o[1] + pi * o[0]).astype(bf16)

    def forward_left(m, part):
        half = jnp.dot(left[part * n : (part + 1) * n, :], xs[m], preferred_element_type=f32)
        hs[m, :, part * n : (part + 1) * n] = half.astype(bf16)

    def forward_right(m, q):
        sp[m, q] = jnp.dot(hs[m], right[:, q * n : (q + 1) * n], preferred_element_type=f32)

    def weigh_rows(win, i):
        s = win[0]
        rows = i % h
        par = i // h
        for q in range(2):
            v = [sp[m, q, i : i + ch, :] for m in range(2)]
            e = v[0] * v[0] + v[1] * v[1]
            inten = e[:, :h] + e[:, h:] + 1.0
            f = 1.0 - frames[s, i : i + ch, q * h : (q + 1) * h].astype(f32) * lax.rsqrt(inten)
            for m in range(2):
                for part in range(2):
                    ws[m, par, part * h + rows : part * h + rows + ch, q * h : (q + 1) * h] = (
                        v[m][:, part * h : (part + 1) * h] * f
                    ).astype(bf16)

    def inverse_left(m, par):
        ib[m, par] = jnp.dot(gl[par], ws[m, par], preferred_element_type=f32)

    def join_rows(m, part, i):
        a = ib[m, 0, part * h + i : part * h + i + ch, :]
        b = ib[m, 1, part * h + i : part * h + i + ch, :]
        up = (a + b).astype(bf16)
        dn = (a - b).astype(bf16)
        for q in range(2):
            hb[m, q, i : i + ch, part * h : (part + 1) * h] = up[:, q * h : (q + 1) * h]
            hb[m, q, h + i : h + i + ch, part * h : (part + 1) * h] = dn[:, q * h : (q + 1) * h]

    def inverse_right(m, q):
        eb[m, q] = jnp.dot(hb[m, q], gr[q], preferred_element_type=f32)

    def add_rows(win, i0):
      for i in range(i0, i0 + ch, 8):
        add_some(win, i)

    def add_some(win, i):
        _, r, cb, sh, _ = win
        ore, oim = patch_rows(win, i, 8)
        acc = None
        for m in range(2):
            e = eb[m, 0, i : i + 8, :]
            d = eb[m, 1, i : i + 8, :]
            up = e + d
            dn = e - d
            bre = jnp.concatenate([up[:, :h], dn[:, :h]], 1)
            bim = jnp.concatenate([up[:, h:], dn[:, h:]], 1)
            pr = probe[m, 0, i : i + 8, :]
            pi = probe[m, 1, i : i + 8, :]
            g = (pr * bre + pi * bim, pr * bim - pi * bre)
            acc = g if m == 0 else (acc[0] + g[0], acc[1] + g[1])
            p_out[m, 0, i : i + 8, :] += ore * bre + oim * bim
            p_out[m, 1, i : i + 8, :] += ore * bim - oim * bre
        zero = jnp.zeros((8, 128), f32)
        v = [pltpu.roll(jnp.concatenate([x, zero], 1), sh, 1) for x in acc]
        new = [
            gext[p, cb + b, pl.ds(r + i, 8), :] + v[p][:, b * 128 : (b + 1) * 128]
            for p in range(2)
            for b in range(3)
        ]
        for p in range(2):
            for b in range(3):
                gext[p, cb + b, pl.ds(r + i, 8), :] = new[p * 3 + b]

    chunks = list(range(0, n, ch))
    pairs = [(m, k) for m in range(2) for k in range(2)]

    def step(t, _):
        now = window(t)
        old = window(t - 1)
        for k, (m, par) in enumerate(pairs):
            inverse_left(m, par)
            for i in chunks[2 * k : 2 * k + 2]:
                wave_rows(now, i)
        for m in range(2):
            for part in range(2):
                for i in range(0, h, ch):
                    join_rows(m, part, i)
        for k, (m, q) in enumerate(pairs):
            inverse_right(m, q)
            for i in chunks[8 + 2 * k : 8 + 2 * k + 2]:
                wave_rows(now, i)
        for k, (m, part) in enumerate(pairs):
            forward_left(m, part)
            for i in chunks[2 * k : 2 * k + 2]:
                add_rows(old, i)
        for k, (m, q) in enumerate(pairs):
            forward_right(m, q)
            for i in chunks[8 + 2 * k : 8 + 2 * k + 2]:
                add_rows(old, i)
        for i in chunks:
            weigh_rows(now, i)

        @pl.when(t == 0)
        def _():
            clear()

        return 0

    lax.fori_loop(0, count + 1, step, 0)


def fill(ext, sources):
    for p in range(2):
        for src, c_from, c_to, r0, c0 in sources:
            for b in range((c_to - c_from) // 128):
                lo = c_from + b * 128
                ext[p, c0 // 128 + b, r0 : r0 + src.shape[1], :] = src[p, :, lo : lo + 128].astype(f32)


def drain(gext, targets):
    for p in range(2):
        for dst, d0, width, r0, c0 in targets:
            for b in range(width // 128):
                dst[p, :, d0 + b * 128 : d0 + (b + 1) * 128] = gext[
                    p, c0 // 128 + b, r0 : r0 + dst.shape[1], :
                ].astype(dst.dtype)


def inner_kernel(
    pos, cnt, own, below, probe, frames, left, right, gl, gr,
    g_own, g_below, carry, p_out,
    ext, gext, *scratch,
):
    n = probe.shape[-1]
    tr, tc = own.shape[1:]
    inner = tc - n
    fill(ext, ((own, 0, tc, 0, 0), (below, 0, tc, tr, 0)))

    def clear():
        gext[...] = jnp.zeros_like(gext)
        p_out[...] = jnp.zeros_like(p_out)

    positions_pass(
        pos, cnt, lambda c: c < inner, 0, tc // 128, clear, probe, frames, (left, right, gl, gr), p_out,
        ext, gext, *scratch,
    )
    drain(gext, ((g_own, 0, inner, 0, 0), (g_below, 0, inner, tr, 0)))
    for p in range(2):
        for b in range(n // 128):
            carry[p, b] = gext[p, inner // 128 + b]


def edge_kernel(
    scale, pos, cnt, own, below, strip, corner, carry, p_in, probe, frames, left, right, gl, gr,
    g_own, g_rows, g_strip, p_out,
    ext, gext, *scratch,
):
    n = probe.shape[-1]
    tr, tc = own.shape[1:]
    inner = tc - n
    fill(
        ext,
        ((own, inner, tc, 0, 0), (below, inner, tc, tr, 0), (strip, 0, n, 0, n), (corner, 0, n, tr, n)),
    )

    def clear():
        p_out[...] = p_in[...]
        for p in range(2):
            for b in range(n // 128):
                gext[p, b] = carry[p, b]
                gext[p, n // 128 + b] = jnp.zeros_like(gext[p, b])

    positions_pass(
        pos, cnt, lambda c: c >= inner, inner // 128, 2 * n // 128, clear, probe, frames,
        (left, right, gl, gr), p_out, ext, gext, *scratch,
    )
    p_out[...] = p_out[...] * scale
    drain(gext, ((g_own, 0, n, 0, 0), (g_rows, 0, 2 * n, tr, 0), (g_strip, 0, n, 0, n)))


def body(object_field, probe, measured, positions, counts):
    size = probe.shape[-1]
    tile_rows, tile_cols = object_field.shape[1:]
    slots = measured.shape[2]
    left, right, gl, gr, perm, perm_t = tables(size)
    vmem = pl.BlockSpec(memory_space=pltpu.VMEM)
    smem = pl.BlockSpec(memory_space=pltpu.SMEM)
    pos, cnt = positions[0, 0], counts[0]
    inner = tile_cols - size
    rows = tile_rows + size

    below = shifted(object_field, "row", -1)
    strip = shifted(object_field[:, :, :size], "col", -1)
    corner = shifted(strip, "row", -1)
    frames = pl.pallas_call(
        prep_kernel,
        out_shape=jax.ShapeDtypeStruct(measured.shape[2:], bf16),
        in_specs=[vmem] * 3,
        out_specs=vmem,
        compiler_params=pltpu.CompilerParams(vmem_limit_bytes=8 * 2**20),
        cost_estimate=pl.CostEstimate(
            flops=slots * 4 * size**3, bytes_accessed=4 * slots * size * size, transcendentals=0
        ),
    )(measured[0, 0], perm, perm_t)

    def scratch(blocks):
        return [
            pltpu.VMEM((2, blocks, rows, 128), f32),
            pltpu.VMEM((2, blocks, rows, 128), f32),
            pltpu.VMEM((2, 2 * size, size), bf16),
            pltpu.VMEM((2, size, 2 * size), bf16),
            pltpu.VMEM((2, 2, size, size), f32),
            pltpu.VMEM((2, 2, size, size), bf16),
            pltpu.VMEM((2, 2, size, size), f32),
            pltpu.VMEM((2, 2, size, size), bf16),
            pltpu.VMEM((2, 2, size, size), f32),
            pltpu.SMEM((slots,), jnp.int32),
        ]

    params = pltpu.CompilerParams(vmem_limit_bytes=32 * 2**20)
    g_main, g_band, carry, p_part = pl.pallas_call(
        inner_kernel,
        out_shape=(
            jax.ShapeDtypeStruct((2, tile_rows, inner), f32),
            jax.ShapeDtypeStruct((2, size, inner), bf16),
            jax.ShapeDtypeStruct((2, size // 128, rows, 128), f32),
            jax.ShapeDtypeStruct(probe.shape, f32),
        ),
        in_specs=[smem, smem] + [vmem] * 8,
        out_specs=[vmem] * 4,
        scratch_shapes=scratch(tile_cols // 128),
        compiler_params=params,
        cost_estimate=pl.CostEstimate(flops=9 * 2**30, bytes_accessed=12 * 2**20, transcendentals=0),
    )(pos, cnt, object_field, below, probe, frames, left, right, gl, gr)
    total = slots * lax.axis_size("row") * lax.axis_size("col")
    scale = 1.0 / math.sqrt(total)
    g_right, g_rows, g_strip, p_sum = pl.pallas_call(
        lambda *refs: edge_kernel(scale, *refs),
        out_shape=(
            jax.ShapeDtypeStruct((2, tile_rows, size), f32),
            jax.ShapeDtypeStruct((2, size, 2 * size), bf16),
            jax.ShapeDtypeStruct((2, tile_rows, size), bf16),
            jax.ShapeDtypeStruct(probe.shape, f32),
        ),
        in_specs=[smem, smem] + [vmem] * 12,
        out_specs=[vmem] * 4,
        scratch_shapes=scratch(2 * size // 128),
        compiler_params=params,
        cost_estimate=pl.CostEstimate(flops=3 * 2**30, bytes_accessed=12 * 2**20, transcendentals=0),
    )(pos, cnt, object_field, below, strip, corner, carry, p_part, probe, frames, left, right, gl, gr)

    band = shifted(g_band, "row", 1)
    tail = shifted(g_rows, "row", 1)
    to_right = (g_strip.astype(f32) + tail[:, :, size:].astype(f32)).astype(bf16)
    side = shifted(to_right, "col", 1)
    probe_grad = reduce_all(p_sum.reshape(-1, size)).reshape(probe.shape)
    object_grad = jnp.concatenate(
        [g_main + band.astype(f32), g_right + tail[:, :, :size].astype(f32)], 2
    )
    object_grad = object_grad.at[:, :, :size].add(side.astype(f32))
    return (object_grad, probe_grad)


def solution(mesh):
    placed = (
        P(None, "row", "col"),
        P(),
        P("row", "col", None, None, None),
        P("row", "col", None, None),
        P("row", "col"),
    )
    return jax.shard_map(
        body, mesh=mesh, in_specs=placed, out_specs=(P(None, "row", "col"), P()), check_vma=False
    )
```

```python
import math

import jax
import jax.numpy as jnp
import numpy as np
from jax import lax
from jax.experimental import pallas as pl
from jax.experimental.pallas import tpu as pltpu
from jax.sharding import PartitionSpec as P


f32 = jnp.float32
bf16 = jnp.bfloat16


def shifted(x, axis, by):
    peers = lax.axis_size(axis)
    pairs = [(i, i + by) for i in range(peers) if 0 <= i + by < peers]
    return lax.ppermute(x, axis, pairs)


FIELDS = {
    "core": ([(1, 0)], 0),
    "y": ([(8, 0), (16, 0), (24, 0)], 3),
    "x": ([(0, 2), (0, 4), (0, 6)], None),
    "z0": ([(2, 0)], None),
    "z1": ([(4, 0)], None),
    "z2": ([(4, 1)], None),
}


def partner(v, field, d):
    row, col = FIELDS[field][0][d - 1]
    if not col:
        return lax.ppermute(v, "row", [(i, i ^ row) for i in range(lax.axis_size("row"))])
    if not row:
        return lax.ppermute(v, "col", [(i, i ^ col) for i in range(lax.axis_size("col"))])
    rows, cols = lax.axis_size("row"), lax.axis_size("col")
    pairs = [(r * cols + c, (r ^ row) * cols + (c ^ col)) for r in range(rows) for c in range(cols)]
    return lax.ppermute(v, ("row", "col"), pairs)


def members(field):
    return len(FIELDS[field][0]) + 1


def place(field):
    return (lax.axis_index("row") >> FIELDS[field][1]) & (members(field) - 1)


def scatter_sum(v, field, dtype):
    n = members(field)
    g = place(field)
    k = v.shape[0] // n
    total = lax.dynamic_slice_in_dim(v, g * k, k, 0)
    got = [
        partner(lax.dynamic_slice_in_dim(v, (g ^ d) * k, k, 0).astype(dtype), field, d)
        for d in range(1, n)
    ]
    for part in got:
        total = total + part.astype(f32)
    return total


def full_sum(v, field, dtype):
    n = members(field)
    sent = v.astype(dtype)
    parts = [sent.astype(f32)] + [partner(sent, field, d).astype(f32) for d in range(1, n)]
    while len(parts) > 1:
        parts = [parts[i] + parts[i + 1] for i in range(0, len(parts), 2)]
    return parts[0]


def gather(v, field, dtype):
    n = members(field)
    g = place(field)
    k = v.shape[0]
    sent = v.astype(dtype)
    got = [partner(sent, field, d) for d in range(1, n)]
    out = jnp.zeros((n * k,) + v.shape[1:], dtype)
    out = lax.dynamic_update_slice_in_dim(out, sent, g * k, 0)
    for d in range(1, n):
        out = lax.dynamic_update_slice_in_dim(out, got[d - 1], (g ^ d) * k, 0)
    return out


PLAN = (
    (scatter_sum, "y", bf16),
    (full_sum, "x", bf16),
    (full_sum, "z0", bf16),
    (full_sum, "z1", bf16),
    (full_sum, "z2", bf16),
    (gather, "y", bf16),
    (gather, "core", bf16),
)


def reduce_all(keep, send):
    v = keep + partner(send, "core", 1).astype(f32)
    for step, field, dtype in PLAN:
        v = step(v, field, dtype)
    return v.astype(f32)


def dft_parts(size):
    index = np.arange(size)
    phase = (index[:, None] * index[None, :]) % size
    angle = 2.0 * np.pi / size * phase
    cosine = (np.cos(angle) / np.sqrt(size)).astype(jnp.bfloat16).astype(np.float32)
    sine = (np.sin(angle) / np.sqrt(size)).astype(jnp.bfloat16).astype(np.float32)
    return cosine, sine


def tables(size):
    half = size // 2
    c, s = dft_parts(size)
    order = np.concatenate([np.arange(0, size, 2), np.arange(1, size, 2)])
    fc, fs = c[order], s[order]
    left = np.block([[fc, fs], [-fs, fc]])
    cols = []
    for q in range(2):
        pick = order[q * half : (q + 1) * half]
        cols.append(np.block([[c[:, pick], -s[:, pick]], [s[:, pick], c[:, pick]]]))
    right = np.concatenate(cols, 1)
    gl, gr = [], []
    for q in range(2):
        ce, se = c[:half, q::2], s[:half, q::2]
        gl.append(np.block([[ce, -se], [se, ce]]))
        cr, sr = c[q::2, :half], s[q::2, :half]
        gr.append(np.block([[cr, sr], [-sr, cr]]))
    perm = np.zeros((size, size), np.float32)
    perm[np.arange(size), order] = 1.0
    to = lambda a: jnp.asarray(np.asarray(a, np.float32).astype(jnp.bfloat16))
    return to(left), to(right), to(np.stack(gl)), to(np.stack(gr)), to(perm), to(perm.T)


def prep_kernel(frames, rows, cols, out):
    def one(s, _):
        a = jnp.dot(rows[...], frames[s], preferred_element_type=f32).astype(bf16)
        out[s] = jnp.dot(a, cols[...], preferred_element_type=f32).astype(bf16)
        return 0

    lax.fori_loop(0, frames.shape[0], one, 0)


def positions_pass(
    pos, cnt, wanted, base, blocks, clear, probe, frames, tables, p_out,
    ext, gext, xs, hs, sp, ws, ib, hb, eb, todo,
):
    left, right, gl, gr = tables
    n = probe.shape[-1]
    h = n // 2
    ch = 16
    todo[0] = 0

    def pick(s, k):
        take = wanted(pos[s, 1])

        @pl.when(take)
        def _():
            todo[k] = s

        return k + take.astype(jnp.int32)

    count = lax.fori_loop(0, cnt[0], pick, 0)
    last = jnp.maximum(count - 1, 0)

    def window(t):
        s = todo[jnp.clip(t, 0, last)]
        c = pos[s, 1]
        sh = lax.rem(c, 128)
        cb = jnp.clip(c // 128 - base, 0, blocks - 3)
        return s, pos[s, 0], cb, sh, lax.rem(384 - sh, 384)

    def patch_rows(win, i, ch=16):
        _, r, cb, _, unshift = win
        out = []
        for p in range(2):
            w = jnp.concatenate([ext[p, cb + b, pl.ds(r + i, ch), :] for b in range(3)], 1)
            out.append(pltpu.roll(w, unshift, 1)[:, :n])
        return out

    def wave_rows(win, i):
        o = patch_rows(win, i)
        for m in range(2):
            pr = probe[m, 0, i : i + ch, :]
            pi = probe[m, 1, i : i + ch, :]
            xs[m, i : i + ch, :] = (pr * o[0] - pi * o[1]).astype(bf16)
            xs[m, n + i : n + i + ch, :] = (pr * o[1] + pi * o[0]).astype(bf16)

    def forward_left(m, part):
        half = jnp.dot(left[part * n : (part + 1) * n, :], xs[m], preferred_element_type=f32)
        hs[m, :, part * n : (part + 1) * n] = half.astype(bf16)

    def forward_right(m, q):
        sp[m, q] = jnp.dot(hs[m], right[:, q * n : (q + 1) * n], preferred_element_type=f32)

    def weigh_rows(win, i):
        s = win[0]
        rows = i % h
        par = i // h
        for q in range(2):
            v = [sp[m, q, i : i + ch, :] for m in range(2)]
            e = v[0] * v[0] + v[1] * v[1]
            inten = e[:, :h] + e[:, h:] + 1.0
            f = 1.0 - frames[s, i : i + ch, q * h : (q + 1) * h].astype(f32) * lax.rsqrt(inten)
            for m in range(2):
                for part in range(2):
                    ws[m, par, part * h + rows : part * h + rows + ch, q * h : (q + 1) * h] = (
                        v[m][:, part * h : (part + 1) * h] * f
                    ).astype(bf16)

    def inverse_left(m, par):
        ib[m, par] = jnp.dot(gl[par], ws[m, par], preferred_element_type=f32)

    def join_rows(m, part, i):
        a = ib[m, 0, part * h + i : part * h + i + ch, :]
        b = ib[m, 1, part * h + i : part * h + i + ch, :]
        up = (a + b).astype(bf16)
        dn = (a - b).astype(bf16)
        for q in range(2):
            hb[m, q, i : i + ch, part * h : (part + 1) * h] = up[:, q * h : (q + 1) * h]
            hb[m, q, h + i : h + i + ch, part * h : (part + 1) * h] = dn[:, q * h : (q + 1) * h]

    def inverse_right(m, q):
        eb[m, q] = jnp.dot(hb[m, q], gr[q], preferred_element_type=f32)

    def add_rows(win, i0):
      for i in range(i0, i0 + ch, 8):
        add_some(win, i)

    def add_some(win, i):
        _, r, cb, sh, _ = win
        ore, oim = patch_rows(win, i, 8)
        acc = None
        for m in range(2):
            e = eb[m, 0, i : i + 8, :]
            d = eb[m, 1, i : i + 8, :]
            up = e + d
            dn = e - d
            bre = jnp.concatenate([up[:, :h], dn[:, :h]], 1)
            bim = jnp.concatenate([up[:, h:], dn[:, h:]], 1)
            pr = probe[m, 0, i : i + 8, :]
            pi = probe[m, 1, i : i + 8, :]
            g = (pr * bre + pi * bim, pr * bim - pi * bre)
            acc = g if m == 0 else (acc[0] + g[0], acc[1] + g[1])
            p_out[m, 0, i : i + 8, :] += ore * bre + oim * bim
            p_out[m, 1, i : i + 8, :] += ore * bim - oim * bre
        zero = jnp.zeros((8, 128), f32)
        v = [pltpu.roll(jnp.concatenate([x, zero], 1), sh, 1) for x in acc]
        new = [
            gext[p, cb + b, pl.ds(r + i, 8), :] + v[p][:, b * 128 : (b + 1) * 128]
            for p in range(2)
            for b in range(3)
        ]
        for p in range(2):
            for b in range(3):
                gext[p, cb + b, pl.ds(r + i, 8), :] = new[p * 3 + b]

    chunks = list(range(0, n, ch))
    pairs = [(m, k) for m in range(2) for k in range(2)]

    def step(t, _):
        now = window(t)
        old = window(t - 1)
        for k, (m, par) in enumerate(pairs):
            inverse_left(m, par)
            for i in chunks[2 * k : 2 * k + 2]:
                wave_rows(now, i)
        for m in range(2):
            for part in range(2):
                for i in range(0, h, ch):
                    join_rows(m, part, i)
        for k, (m, q) in enumerate(pairs):
            inverse_right(m, q)
            for i in chunks[8 + 2 * k : 8 + 2 * k + 2]:
                wave_rows(now, i)
        for k, (m, part) in enumerate(pairs):
            forward_left(m, part)
            for i in chunks[2 * k : 2 * k + 2]:
                add_rows(old, i)
        for k, (m, q) in enumerate(pairs):
            forward_right(m, q)
            for i in chunks[8 + 2 * k : 8 + 2 * k + 2]:
                add_rows(old, i)
        for i in chunks:
            weigh_rows(now, i)

        @pl.when(t == 0)
        def _():
            clear()

        return 0

    lax.fori_loop(0, count + 1, step, 0)


def fill(ext, sources):
    for p in range(2):
        for src, c_from, c_to, r0, c0 in sources:
            for b in range((c_to - c_from) // 128):
                lo = c_from + b * 128
                ext[p, c0 // 128 + b, r0 : r0 + src.shape[1], :] = src[p, :, lo : lo + 128].astype(f32)


def drain(gext, targets):
    for p in range(2):
        for dst, d0, width, r0, c0 in targets:
            for b in range(width // 128):
                dst[p, :, d0 + b * 128 : d0 + (b + 1) * 128] = gext[
                    p, c0 // 128 + b, r0 : r0 + dst.shape[1], :
                ].astype(dst.dtype)


def fetch(sources, targets, sems):
    copies = [pltpu.make_async_copy(s, d, sems.at[k]) for k, (s, d) in enumerate(zip(sources, targets))]
    for copy in copies:
        copy.start()
    return copies


def inner_kernel(
    pos, cnt, own_hbm, below_hbm, probe_hbm, frames_hbm, left_hbm, right_hbm, gl_hbm, gr_hbm,
    g_own, g_below, carry, p_out,
    own, below, probe, frames, left, right, gl, gr, sems, ext, gext, *scratch,
):
    copies = fetch(
        (own_hbm, below_hbm, probe_hbm, left_hbm, right_hbm, gl_hbm, gr_hbm, frames_hbm),
        (own, below, probe, left, right, gl, gr, frames),
        sems,
    )
    n = probe.shape[-1]
    tr, tc = own.shape[1:]
    inner = tc - n
    copies[0].wait()
    fill(ext, ((own, 0, tc, 0, 0),))
    copies[1].wait()
    fill(ext, ((below, 0, tc, tr, 0),))
    for copy in copies[2:]:
        copy.wait()

    def clear():
        gext[...] = jnp.zeros_like(gext)
        p_out[...] = jnp.zeros_like(p_out)

    positions_pass(
        pos, cnt, lambda c: c < inner, 0, tc // 128, clear, probe, frames, (left, right, gl, gr), p_out,
        ext, gext, *scratch,
    )
    drain(gext, ((g_own, 0, inner, 0, 0), (g_below, 0, inner, tr, 0)))
    for p in range(2):
        for b in range(n // 128):
            carry[p, b] = gext[p, inner // 128 + b]


def edge_kernel(
    scale, pos, cnt, core, own_hbm, below_hbm, strip_hbm, corner_hbm, carry_hbm, p_hbm, probe_hbm, frames_hbm,
    left_hbm, right_hbm, gl_hbm, gr_hbm,
    g_own, g_rows, g_strip, p_keep, p_send,
    own, below, strip, corner, carry, p_in, probe, frames, left, right, gl, gr, sems, p_out, ext, gext, *scratch,
):
    n = probe.shape[-1]
    tr, tc = own_hbm.shape[1:]
    inner = tc - n
    copies = fetch(
        (
            own_hbm.at[:, :, inner:tc], below_hbm.at[:, :, inner:tc], strip_hbm, corner_hbm, probe_hbm,
            left_hbm, right_hbm, gl_hbm, gr_hbm, frames_hbm, p_hbm, carry_hbm,
        ),
        (own, below, strip, corner, probe, left, right, gl, gr, frames, p_in, carry),
        sems,
    )
    for copy in copies[:4]:
        copy.wait()
    fill(ext, ((own, 0, n, 0, 0), (below, 0, n, tr, 0), (strip, 0, n, 0, n), (corner, 0, n, tr, n)))
    for copy in copies[4:10]:
        copy.wait()

    def clear():
        for copy in copies[10:]:
            copy.wait()
        p_out[...] = p_in[...]
        for p in range(2):
            for b in range(n // 128):
                gext[p, b] = carry[p, b]
                gext[p, n // 128 + b] = jnp.zeros_like(gext[p, b])

    positions_pass(
        pos, cnt, lambda c: c >= inner, inner // 128, 2 * n // 128, clear, probe, frames,
        (left, right, gl, gr), p_out, ext, gext, *scratch,
    )
    p_keep[...] = p_out[core[0]] * scale
    p_send[...] = (p_out[1 - core[0]] * scale).astype(bf16)
    drain(gext, ((g_own, 0, n, 0, 0), (g_rows, 0, 2 * n, tr, 0), (g_strip, 0, n, 0, n)))


def body(object_field, probe, measured, positions, counts):
    size = probe.shape[-1]
    tile_rows, tile_cols = object_field.shape[1:]
    slots = measured.shape[2]
    left, right, gl, gr, perm, perm_t = tables(size)
    vmem = pl.BlockSpec(memory_space=pltpu.VMEM)
    stay = pl.BlockSpec(memory_space=pl.ANY)
    smem = pl.BlockSpec(memory_space=pltpu.SMEM)
    pos, cnt = positions[0, 0], counts[0]
    core = (lax.axis_index("row") & 1).astype(jnp.int32).reshape(1)
    inner = tile_cols - size
    rows = tile_rows + size

    below = shifted(object_field, "row", -1)
    strip = shifted(object_field[:, :, :size], "col", -1)
    corner = shifted(strip, "row", -1)
    frames = pl.pallas_call(
        prep_kernel,
        out_shape=jax.ShapeDtypeStruct(measured.shape[2:], bf16),
        in_specs=[vmem] * 3,
        out_specs=vmem,
        compiler_params=pltpu.CompilerParams(vmem_limit_bytes=8 * 2**20),
        cost_estimate=pl.CostEstimate(
            flops=slots * 4 * size**3, bytes_accessed=4 * slots * size * size, transcendentals=0
        ),
    )(measured[0, 0], perm, perm_t)

    def scratch(blocks):
        return [
            pltpu.VMEM((2, blocks, rows, 128), f32),
            pltpu.VMEM((2, blocks, rows, 128), f32),
            pltpu.VMEM((2, 2 * size, size), bf16),
            pltpu.VMEM((2, size, 2 * size), bf16),
            pltpu.VMEM((2, 2, size, size), f32),
            pltpu.VMEM((2, 2, size, size), bf16),
            pltpu.VMEM((2, 2, size, size), f32),
            pltpu.VMEM((2, 2, size, size), bf16),
            pltpu.VMEM((2, 2, size, size), f32),
            pltpu.SMEM((slots,), jnp.int32),
        ]

    fixed = [pltpu.VMEM(x.shape, x.dtype) for x in (probe, frames, left, right, gl, gr)]
    params = pltpu.CompilerParams(vmem_limit_bytes=60 * 2**20)
    g_main, g_band, carry, p_part = pl.pallas_call(
        inner_kernel,
        out_shape=(
            jax.ShapeDtypeStruct((2, tile_rows, inner), f32),
            jax.ShapeDtypeStruct((2, size, inner), bf16),
            jax.ShapeDtypeStruct((2, size // 128, rows, 128), f32),
            jax.ShapeDtypeStruct(probe.shape, f32),
        ),
        in_specs=[smem, smem] + [stay] * 8,
        out_specs=[vmem] * 4,
        scratch_shapes=[
            pltpu.VMEM((2, tile_rows, tile_cols), bf16),
            pltpu.VMEM((2, size, tile_cols), bf16),
        ]
        + fixed
        + [pltpu.SemaphoreType.DMA((8,))]
        + scratch(tile_cols // 128),
        compiler_params=params,
        cost_estimate=pl.CostEstimate(flops=9 * 2**30, bytes_accessed=12 * 2**20, transcendentals=0),
    )(pos, cnt, object_field, below, probe, frames, left, right, gl, gr)
    total = slots * lax.axis_size("row") * lax.axis_size("col")
    scale = 1.0 / math.sqrt(total)
    g_right, g_rows, g_strip, p_keep, p_send = pl.pallas_call(
        lambda *refs: edge_kernel(scale, *refs),
        out_shape=(
            jax.ShapeDtypeStruct((2, tile_rows, size), f32),
            jax.ShapeDtypeStruct((2, size, 2 * size), bf16),
            jax.ShapeDtypeStruct((2, tile_rows, size), bf16),
            jax.ShapeDtypeStruct(probe.shape[1:], f32),
            jax.ShapeDtypeStruct(probe.shape[1:], bf16),
        ),
        in_specs=[smem] * 3 + [stay] * 12,
        out_specs=[vmem] * 5,
        scratch_shapes=[
            pltpu.VMEM((2, tile_rows, size), bf16),
            pltpu.VMEM((2, size, size), bf16),
            pltpu.VMEM((2, tile_rows, size), bf16),
            pltpu.VMEM((2, size, size), bf16),
            pltpu.VMEM((2, size // 128, rows, 128), f32),
            pltpu.VMEM(probe.shape, f32),
        ]
        + fixed
        + [pltpu.SemaphoreType.DMA((12,)), pltpu.VMEM(probe.shape, f32)]
        + scratch(2 * size // 128),
        compiler_params=params,
        cost_estimate=pl.CostEstimate(flops=3 * 2**30, bytes_accessed=12 * 2**20, transcendentals=0),
    )(pos, cnt, core, object_field, below, strip, corner, carry, p_part, probe, frames, left, right, gl, gr)

    band = shifted(g_band, "row", 1)
    tail = shifted(g_rows, "row", 1)
    to_right = (g_strip.astype(f32) + tail[:, :, size:].astype(f32)).astype(bf16)
    side = shifted(to_right, "col", 1)
    probe_grad = reduce_all(p_keep.reshape(-1, size), p_send.reshape(-1, size)).reshape(probe.shape)
    object_grad = jnp.concatenate(
        [g_main + band.astype(f32), g_right + tail[:, :, :size].astype(f32)], 2
    )
    object_grad = object_grad.at[:, :, :size].add(side.astype(f32))
    return (object_grad, probe_grad)


def solution(mesh):
    placed = (
        P(None, "row", "col"),
        P(),
        P("row", "col", None, None, None),
        P("row", "col", None, None),
        P("row", "col"),
    )
    return jax.shard_map(
        body, mesh=mesh, in_specs=placed, out_specs=(P(None, "row", "col"), P()), check_vma=False
    )
```

```python
import math

import jax
import jax.numpy as jnp
import numpy as np
from jax import lax
from jax.experimental import pallas as pl
from jax.experimental.pallas import tpu as pltpu
from jax.sharding import PartitionSpec as P


f32 = jnp.float32
bf16 = jnp.bfloat16


def shifted(x, axis, by):
    peers = lax.axis_size(axis)
    pairs = [(i, i + by) for i in range(peers) if 0 <= i + by < peers]
    return lax.ppermute(x, axis, pairs)


Y = [(8, 0), (16, 0), (24, 0)]
X = [(0, 2), (0, 4), (0, 6)]
FIELDS = {
    "core": ([(1, 0)], [(1, 0)]),
    "first": (Y, X),
    "second": (X, Y),
    "z0": ([(2, 0)], [(2, 0)]),
    "z1": ([(4, 0)], [(4, 0)]),
    "z2": ([(4, 1)], [(4, 1)]),
}


def partner(v, field, d):
    masks = [masks[d - 1] for masks in FIELDS[field]]
    rows, cols = lax.axis_size("row"), lax.axis_size("col")
    pairs = []
    for r in range(rows):
        for c in range(cols):
            row, col = masks[r & 1]
            pairs.append((r * cols + c, (r ^ row) * cols + (c ^ col)))
    return lax.ppermute(v, ("row", "col"), pairs)


def members(field):
    return len(FIELDS[field][0]) + 1


def place(field):
    if field == "core":
        return lax.axis_index("row") & 1
    return jnp.where(lax.axis_index("row") & 1 == 0, lax.axis_index("row") >> 3, lax.axis_index("col") >> 1)


def scatter_sum(v, field, dtype):
    n = members(field)
    g = place(field)
    k = v.shape[0] // n
    total = lax.dynamic_slice_in_dim(v, g * k, k, 0)
    got = [
        partner(lax.dynamic_slice_in_dim(v, (g ^ d) * k, k, 0).astype(dtype), field, d)
        for d in range(1, n)
    ]
    for part in got:
        total = total + part.astype(f32)
    return total


def full_sum(v, field, dtype):
    n = members(field)
    sent = v.astype(dtype)
    parts = [sent.astype(f32)] + [partner(sent, field, d).astype(f32) for d in range(1, n)]
    while len(parts) > 1:
        parts = [parts[i] + parts[i + 1] for i in range(0, len(parts), 2)]
    return parts[0]


def gather(v, field, dtype):
    n = members(field)
    g = place(field)
    k = v.shape[0]
    sent = v.astype(dtype)
    got = [partner(sent, field, d) for d in range(1, n)]
    out = jnp.zeros((n * k,) + v.shape[1:], dtype)
    out = lax.dynamic_update_slice_in_dim(out, sent, g * k, 0)
    for d in range(1, n):
        out = lax.dynamic_update_slice_in_dim(out, got[d - 1], (g ^ d) * k, 0)
    return out


PLAN = (
    (scatter_sum, "first", bf16),
    (full_sum, "z0", bf16),
    (full_sum, "z1", bf16),
    (full_sum, "z2", bf16),
    (full_sum, "second", bf16),
    (gather, "first", bf16),
    (gather, "core", bf16),
)


def reduce_all(keep, send):
    v = keep + partner(send, "core", 1).astype(f32)
    for step, field, dtype in PLAN:
        v = step(v, field, dtype)
    return v.astype(f32)


def dft_parts(size):
    index = np.arange(size)
    phase = (index[:, None] * index[None, :]) % size
    angle = 2.0 * np.pi / size * phase
    cosine = (np.cos(angle) / np.sqrt(size)).astype(jnp.bfloat16).astype(np.float32)
    sine = (np.sin(angle) / np.sqrt(size)).astype(jnp.bfloat16).astype(np.float32)
    return cosine, sine


def tables(size):
    half = size // 2
    c, s = dft_parts(size)
    order = np.concatenate([np.arange(0, size, 2), np.arange(1, size, 2)])
    fc, fs = c[order], s[order]
    left = np.block([[fc, fs], [-fs, fc]])
    cols = []
    for q in range(2):
        pick = order[q * half : (q + 1) * half]
        cols.append(np.block([[c[:, pick], -s[:, pick]], [s[:, pick], c[:, pick]]]))
    right = np.concatenate(cols, 1)
    gl, gr = [], []
    for q in range(2):
        ce, se = c[:half, q::2], s[:half, q::2]
        gl.append(np.block([[ce, -se], [se, ce]]))
        cr, sr = c[q::2, :half], s[q::2, :half]
        gr.append(np.block([[cr, sr], [-sr, cr]]))
    perm = np.zeros((size, size), np.float32)
    perm[np.arange(size), order] = 1.0
    to = lambda a: jnp.asarray(np.asarray(a, np.float32).astype(jnp.bfloat16))
    return to(left), to(right), to(np.stack(gl)), to(np.stack(gr)), to(perm), to(perm.T)


def prep_kernel(frames, rows, cols, out):
    def one(s, _):
        a = jnp.dot(rows[...], frames[s], preferred_element_type=f32).astype(bf16)
        out[s] = jnp.dot(a, cols[...], preferred_element_type=f32).astype(bf16)
        return 0

    lax.fori_loop(0, frames.shape[0], one, 0)


def choose(pos, cnt, wanted, todo, frames_hbm, frames, sem):
    todo[0] = 0

    def pick(s, k):
        take = wanted(pos[s, 1])

        @pl.when(take)
        def _():
            todo[k] = s
            pltpu.make_async_copy(frames_hbm.at[s], frames.at[s], sem.at[s]).start()

        return k + take.astype(jnp.int32)

    return lax.fori_loop(0, cnt[0], pick, 0)


def await_frames(count, todo, frames_hbm, frames, sem):
    def one(k, _):
        s = todo[k]
        pltpu.make_async_copy(frames_hbm.at[s], frames.at[s], sem.at[s]).wait()
        return 0

    lax.fori_loop(0, count, one, 0)


def positions_pass(
    pos, count, base, blocks, clear, probe, frames, tables, p_out,
    ext, gext, pat, xs, hs, sp, ws, ib, hb, eb, todo,
):
    left, right, gl, gr = tables
    n = probe.shape[-1]
    h = n // 2
    ch = 16
    last = jnp.maximum(count - 1, 0)

    def window(t):
        s = todo[jnp.clip(t, 0, last)]
        c = pos[s, 1]
        sh = lax.rem(c, 128)
        cb = jnp.clip(c // 128 - base, 0, blocks - 3)
        return s, pos[s, 0], cb, sh, lax.rem(384 - sh, 384)

    def patch_rows(win, i, ch=16):
        _, r, cb, _, unshift = win
        out = []
        for p in range(2):
            w = jnp.concatenate([ext[p, cb + b, pl.ds(r + i, ch), :] for b in range(3)], 1)
            out.append(pltpu.roll(w, unshift, 1)[:, :n])
        return out

    def wave_rows(win, slot, i):
        o = patch_rows(win, i)
        for p in range(2):
            pat[slot, p, i : i + ch, :] = o[p]
        for m in range(2):
            pr = probe[m, 0, i : i + ch, :]
            pi = probe[m, 1, i : i + ch, :]
            xs[m, i : i + ch, :] = (pr * o[0] - pi * o[1]).astype(bf16)
            xs[m, n + i : n + i + ch, :] = (pr * o[1] + pi * o[0]).astype(bf16)

    def forward_left(m, part):
        half = jnp.dot(left[part * n : (part + 1) * n, :], xs[m], preferred_element_type=f32)
        hs[m, :, part * n : (part + 1) * n] = half.astype(bf16)

    def forward_right(m, q):
        sp[m, q] = jnp.dot(hs[m], right[:, q * n : (q + 1) * n], preferred_element_type=f32)

    def weigh_rows(win, q, i):
        s = win[0]
        rows = i % h
        par = i // h
        v = [sp[m, q, i : i + ch, :] for m in range(2)]
        e = v[0] * v[0] + v[1] * v[1]
        inten = e[:, :h] + e[:, h:] + 1.0
        f = 1.0 - frames[s, i : i + ch, q * h : (q + 1) * h].astype(f32) * lax.rsqrt(inten)
        for m in range(2):
            for part in range(2):
                ws[m, par, part * h + rows : part * h + rows + ch, q * h : (q + 1) * h] = (
                    v[m][:, part * h : (part + 1) * h] * f
                ).astype(bf16)

    def inverse_left(m, par):
        ib[m, par] = jnp.dot(gl[par], ws[m, par], preferred_element_type=f32)

    def join_rows(m, part, i):
        a = ib[m, 0, part * h + i : part * h + i + ch, :]
        b = ib[m, 1, part * h + i : part * h + i + ch, :]
        up = (a + b).astype(bf16)
        dn = (a - b).astype(bf16)
        for q in range(2):
            hb[m, q, i : i + ch, part * h : (part + 1) * h] = up[:, q * h : (q + 1) * h]
            hb[m, q, h + i : h + i + ch, part * h : (part + 1) * h] = dn[:, q * h : (q + 1) * h]

    def inverse_right(m, q):
        eb[m, q] = jnp.dot(hb[m, q], gr[q], preferred_element_type=f32)

    def add_rows(win, slot, i0):
        for i in range(i0, i0 + ch, 8):
            add_some(win, slot, i)

    def add_some(win, slot, i):
        _, r, cb, sh, _ = win
        ore = pat[slot, 0, i : i + 8, :]
        oim = pat[slot, 1, i : i + 8, :]
        acc = None
        for m in range(2):
            e = eb[m, 0, i : i + 8, :]
            d = eb[m, 1, i : i + 8, :]
            up = e + d
            dn = e - d
            bre = jnp.concatenate([up[:, :h], dn[:, :h]], 1)
            bim = jnp.concatenate([up[:, h:], dn[:, h:]], 1)
            pr = probe[m, 0, i : i + 8, :]
            pi = probe[m, 1, i : i + 8, :]
            g = (pr * bre + pi * bim, pr * bim - pi * bre)
            acc = g if m == 0 else (acc[0] + g[0], acc[1] + g[1])
            p_out[m, 0, i : i + 8, :] += ore * bre + oim * bim
            p_out[m, 1, i : i + 8, :] += ore * bim - oim * bre
        zero = jnp.zeros((8, 128), f32)
        v = [pltpu.roll(jnp.concatenate([x, zero], 1), sh, 1) for x in acc]
        new = [
            gext[p, cb + b, pl.ds(r + i, 8), :] + v[p][:, b * 128 : (b + 1) * 128]
            for p in range(2)
            for b in range(3)
        ]
        for p in range(2):
            for b in range(3):
                gext[p, cb + b, pl.ds(r + i, 8), :] = new[p * 3 + b]

    chunks = list(range(0, n, ch))
    pairs = [(m, k) for m in range(2) for k in range(2)]

    def step(t, _):
        now = window(t)
        old = window(t - 1)
        new_slot = lax.rem(t, 2)
        old_slot = 1 - new_slot
        for k, (m, par) in enumerate(pairs):
            inverse_left(m, par)
            for i in chunks[2 * k : 2 * k + 2]:
                wave_rows(now, new_slot, i)
        for m in range(2):
            for part in range(2):
                for i in range(0, h, ch):
                    join_rows(m, part, i)
        for k, (m, q) in enumerate(pairs):
            inverse_right(m, q)
            for i in chunks[8 + 2 * k : 8 + 2 * k + 2]:
                wave_rows(now, new_slot, i)
        for k, (m, part) in enumerate(pairs):
            forward_left(m, part)
            for i in chunks[3 * k : 3 * k + 3]:
                add_rows(old, old_slot, i)
        for m in range(2):
            forward_right(m, 0)
            for i in chunks[12 + 2 * m : 12 + 2 * m + 2]:
                add_rows(old, old_slot, i)
        for m in range(2):
            forward_right(m, 1)
            for i in chunks[8 * m : 8 * m + 8]:
                weigh_rows(now, 0, i)
        for i in chunks:
            weigh_rows(now, 1, i)

        @pl.when(t == 0)
        def _():
            clear()

        return 0

    lax.fori_loop(0, count + 1, step, 0)


def fill(ext, sources):
    for p in range(2):
        for src, c_from, c_to, r0, c0 in sources:
            for b in range((c_to - c_from) // 128):
                lo = c_from + b * 128
                ext[p, c0 // 128 + b, r0 : r0 + src.shape[1], :] = src[p, :, lo : lo + 128].astype(f32)


def drain(gext, targets):
    for p in range(2):
        for dst, d0, width, r0, c0 in targets:
            for b in range(width // 128):
                dst[p, :, d0 + b * 128 : d0 + (b + 1) * 128] = gext[
                    p, c0 // 128 + b, r0 : r0 + dst.shape[1], :
                ].astype(dst.dtype)


def fetch(sources, targets, sems):
    copies = [pltpu.make_async_copy(s, d, sems.at[k]) for k, (s, d) in enumerate(zip(sources, targets))]
    for copy in copies:
        copy.start()
    return copies


def inner_kernel(
    pos, cnt, own_hbm, below_hbm, probe_hbm, frames_hbm, left_hbm, right_hbm, gl_hbm, gr_hbm,
    g_own, g_below, carry, p_out,
    own, below, probe, frames, left, right, gl, gr, sems, frame_sems, ext, gext, *scratch,
):
    copies = fetch(
        (own_hbm, below_hbm, probe_hbm, left_hbm, right_hbm, gl_hbm, gr_hbm),
        (own, below, probe, left, right, gl, gr),
        sems,
    )
    n = probe.shape[-1]
    tr, tc = own.shape[1:]
    inner = tc - n
    todo = scratch[-1]
    count = choose(pos, cnt, lambda c: c < inner, todo, frames_hbm, frames, frame_sems)
    copies[0].wait()
    fill(ext, ((own, 0, tc, 0, 0),))
    copies[1].wait()
    fill(ext, ((below, 0, tc, tr, 0),))
    for copy in copies[2:]:
        copy.wait()
    await_frames(count, todo, frames_hbm, frames, frame_sems)

    def clear():
        gext[...] = jnp.zeros_like(gext)
        p_out[...] = jnp.zeros_like(p_out)

    positions_pass(
        pos, count, 0, tc // 128, clear, probe, frames, (left, right, gl, gr), p_out,
        ext, gext, *scratch,
    )
    drain(gext, ((g_own, 0, inner, 0, 0), (g_below, 0, inner, tr, 0)))
    for p in range(2):
        for b in range(n // 128):
            carry[p, b] = gext[p, inner // 128 + b]


def edge_kernel(
    scale, pos, cnt, core, own_hbm, below_hbm, strip_hbm, corner_hbm, carry_hbm, p_hbm, probe_hbm, frames_hbm,
    left_hbm, right_hbm, gl_hbm, gr_hbm,
    g_own, g_rows, g_strip, p_keep, p_send,
    own, below, strip, corner, carry, p_in, probe, frames, left, right, gl, gr, sems, frame_sems, p_out, ext, gext, *scratch,
):
    n = probe.shape[-1]
    tr, tc = own_hbm.shape[1:]
    inner = tc - n
    copies = fetch(
        (
            own_hbm.at[:, :, inner:tc], below_hbm.at[:, :, inner:tc], strip_hbm, corner_hbm, probe_hbm,
            left_hbm, right_hbm, gl_hbm, gr_hbm, p_hbm, carry_hbm,
        ),
        (own, below, strip, corner, probe, left, right, gl, gr, p_in, carry),
        sems,
    )
    todo = scratch[-1]
    count = choose(pos, cnt, lambda c: c >= inner, todo, frames_hbm, frames, frame_sems)
    for copy in copies[:4]:
        copy.wait()
    fill(ext, ((own, 0, n, 0, 0), (below, 0, n, tr, 0), (strip, 0, n, 0, n), (corner, 0, n, tr, n)))
    for copy in copies[4:9]:
        copy.wait()
    await_frames(count, todo, frames_hbm, frames, frame_sems)

    def clear():
        for copy in copies[9:]:
            copy.wait()
        p_out[...] = p_in[...]
        for p in range(2):
            for b in range(n // 128):
                gext[p, b] = carry[p, b]
                gext[p, n // 128 + b] = jnp.zeros_like(gext[p, b])

    positions_pass(
        pos, count, inner // 128, 2 * n // 128, clear, probe, frames,
        (left, right, gl, gr), p_out, ext, gext, *scratch,
    )
    p_keep[...] = p_out[core[0]] * scale
    p_send[...] = (p_out[1 - core[0]] * scale).astype(bf16)
    drain(gext, ((g_own, 0, n, 0, 0), (g_rows, 0, 2 * n, tr, 0), (g_strip, 0, n, 0, n)))


def body(object_field, probe, measured, positions, counts):
    size = probe.shape[-1]
    tile_rows, tile_cols = object_field.shape[1:]
    slots = measured.shape[2]
    left, right, gl, gr, perm, perm_t = tables(size)
    vmem = pl.BlockSpec(memory_space=pltpu.VMEM)
    stay = pl.BlockSpec(memory_space=pl.ANY)
    smem = pl.BlockSpec(memory_space=pltpu.SMEM)
    pos, cnt = positions[0, 0], counts[0]
    core = (lax.axis_index("row") & 1).astype(jnp.int32).reshape(1)
    inner = tile_cols - size
    rows = tile_rows + size

    below = shifted(object_field, "row", -1)
    strip = shifted(object_field[:, :, :size], "col", -1)
    corner = shifted(strip, "row", -1)
    frames = pl.pallas_call(
        prep_kernel,
        out_shape=jax.ShapeDtypeStruct(measured.shape[2:], bf16),
        in_specs=[vmem] * 3,
        out_specs=vmem,
        compiler_params=pltpu.CompilerParams(vmem_limit_bytes=8 * 2**20),
        cost_estimate=pl.CostEstimate(
            flops=slots * 4 * size**3, bytes_accessed=4 * slots * size * size, transcendentals=0
        ),
    )(measured[0, 0], perm, perm_t)

    def scratch(blocks):
        return [
            pltpu.VMEM((2, blocks, rows, 128), f32),
            pltpu.VMEM((2, blocks, rows, 128), f32),
            pltpu.VMEM((2, 2, size, size), f32),
            pltpu.VMEM((2, 2 * size, size), bf16),
            pltpu.VMEM((2, size, 2 * size), bf16),
            pltpu.VMEM((2, 2, size, size), f32),
            pltpu.VMEM((2, 2, size, size), bf16),
            pltpu.VMEM((2, 2, size, size), f32),
            pltpu.VMEM((2, 2, size, size), bf16),
            pltpu.VMEM((2, 2, size, size), f32),
            pltpu.SMEM((slots,), jnp.int32),
        ]

    fixed = [pltpu.VMEM(x.shape, x.dtype) for x in (probe, frames, left, right, gl, gr)]
    params = pltpu.CompilerParams(
        vmem_limit_bytes=60 * 2**20
    )
    g_main, g_band, carry, p_part = pl.pallas_call(
        inner_kernel,
        out_shape=(
            jax.ShapeDtypeStruct((2, tile_rows, inner), f32),
            jax.ShapeDtypeStruct((2, size, inner), bf16),
            jax.ShapeDtypeStruct((2, size // 128, rows, 128), f32),
            jax.ShapeDtypeStruct(probe.shape, f32),
        ),
        in_specs=[smem, smem] + [stay] * 8,
        out_specs=[vmem] * 4,
        scratch_shapes=[
            pltpu.VMEM((2, tile_rows, tile_cols), bf16),
            pltpu.VMEM((2, size, tile_cols), bf16),
        ]
        + fixed
        + [pltpu.SemaphoreType.DMA((7,)), pltpu.SemaphoreType.DMA((slots,))]
        + scratch(tile_cols // 128),
        compiler_params=params,
        cost_estimate=pl.CostEstimate(flops=9 * 2**30, bytes_accessed=12 * 2**20, transcendentals=0),
    )(pos, cnt, object_field, below, probe, frames, left, right, gl, gr)
    total = slots * lax.axis_size("row") * lax.axis_size("col")
    scale = 1.0 / math.sqrt(total)
    g_right, g_rows, g_strip, p_keep, p_send = pl.pallas_call(
        lambda *refs: edge_kernel(scale, *refs),
        out_shape=(
            jax.ShapeDtypeStruct((2, tile_rows, size), f32),
            jax.ShapeDtypeStruct((2, size, 2 * size), bf16),
            jax.ShapeDtypeStruct((2, tile_rows, size), bf16),
            jax.ShapeDtypeStruct(probe.shape[1:], f32),
            jax.ShapeDtypeStruct(probe.shape[1:], bf16),
        ),
        in_specs=[smem] * 3 + [stay] * 12,
        out_specs=[vmem] * 5,
        scratch_shapes=[
            pltpu.VMEM((2, tile_rows, size), bf16),
            pltpu.VMEM((2, size, size), bf16),
            pltpu.VMEM((2, tile_rows, size), bf16),
            pltpu.VMEM((2, size, size), bf16),
            pltpu.VMEM((2, size // 128, rows, 128), f32),
            pltpu.VMEM(probe.shape, f32),
        ]
        + fixed
        + [pltpu.SemaphoreType.DMA((11,)), pltpu.SemaphoreType.DMA((slots,)), pltpu.VMEM(probe.shape, f32)]
        + scratch(2 * size // 128),
        compiler_params=params,
        cost_estimate=pl.CostEstimate(flops=3 * 2**30, bytes_accessed=12 * 2**20, transcendentals=0),
    )(pos, cnt, core, object_field, below, strip, corner, carry, p_part, probe, frames, left, right, gl, gr)

    band = shifted(g_band, "row", 1)
    tail = shifted(g_rows, "row", 1)
    to_right = (g_strip.astype(f32) + tail[:, :, size:].astype(f32)).astype(bf16)
    side = shifted(to_right, "col", 1)
    probe_grad = reduce_all(p_keep.reshape(-1, size), p_send.reshape(-1, size)).reshape(probe.shape)
    object_grad = jnp.concatenate(
        [g_main + band.astype(f32), g_right + tail[:, :, :size].astype(f32)], 2
    )
    object_grad = object_grad.at[:, :, :size].add(side.astype(f32))
    return (object_grad, probe_grad)


def solution(mesh):
    placed = (
        P(None, "row", "col"),
        P(),
        P("row", "col", None, None, None),
        P("row", "col", None, None),
        P("row", "col"),
    )
    return jax.shard_map(
        body, mesh=mesh, in_specs=placed, out_specs=(P(None, "row", "col"), P()), check_vma=False
    )
```

```python
import math

import jax
import jax.numpy as jnp
import numpy as np
from jax import lax
from jax.experimental import pallas as pl
from jax.experimental.pallas import tpu as pltpu
from jax.sharding import PartitionSpec as P


f32 = jnp.float32
bf16 = jnp.bfloat16


def shifted(x, axis, by):
    peers = lax.axis_size(axis)
    pairs = [(i, i + by) for i in range(peers) if 0 <= i + by < peers]
    return lax.ppermute(x, axis, pairs)


Y = [(8, 0), (16, 0), (24, 0)]
X = [(0, 2), (0, 4), (0, 6)]
FIELDS = {
    "core": ([(1, 0)], [(1, 0)]),
    "first": (Y, X),
    "second": (X, Y),
    "z0": ([(2, 0)], [(2, 0)]),
    "z1": ([(4, 0)], [(4, 0)]),
    "z2": ([(4, 1)], [(4, 1)]),
}


def partner(v, field, d):
    masks = [masks[d - 1] for masks in FIELDS[field]]
    rows, cols = lax.axis_size("row"), lax.axis_size("col")
    pairs = []
    for r in range(rows):
        for c in range(cols):
            row, col = masks[r & 1]
            pairs.append((r * cols + c, (r ^ row) * cols + (c ^ col)))
    return lax.ppermute(v, ("row", "col"), pairs)


def members(field):
    return len(FIELDS[field][0]) + 1


def place(field):
    if field == "core":
        return lax.axis_index("row") & 1
    return jnp.where(lax.axis_index("row") & 1 == 0, lax.axis_index("row") >> 3, lax.axis_index("col") >> 1)


def scatter_sum(v, field, dtype):
    n = members(field)
    g = place(field)
    k = v.shape[0] // n
    total = lax.dynamic_slice_in_dim(v, g * k, k, 0)
    got = [
        partner(lax.dynamic_slice_in_dim(v, (g ^ d) * k, k, 0).astype(dtype), field, d)
        for d in range(1, n)
    ]
    for part in got:
        total = total + part.astype(f32)
    return total


def full_sum(v, field, dtype):
    n = members(field)
    sent = v.astype(dtype)
    parts = [sent.astype(f32)] + [partner(sent, field, d).astype(f32) for d in range(1, n)]
    while len(parts) > 1:
        parts = [parts[i] + parts[i + 1] for i in range(0, len(parts), 2)]
    return parts[0]


def gather(v, field, dtype):
    n = members(field)
    g = place(field)
    k = v.shape[0]
    sent = v.astype(dtype)
    got = [partner(sent, field, d) for d in range(1, n)]
    out = jnp.zeros((n * k,) + v.shape[1:], dtype)
    out = lax.dynamic_update_slice_in_dim(out, sent, g * k, 0)
    for d in range(1, n):
        out = lax.dynamic_update_slice_in_dim(out, got[d - 1], (g ^ d) * k, 0)
    return out


PLAN = (
    (scatter_sum, "first", bf16),
    (full_sum, "z0", bf16),
    (full_sum, "z1", bf16),
    (full_sum, "z2", bf16),
    (full_sum, "second", bf16),
    (gather, "first", bf16),
    (gather, "core", bf16),
)


def reduce_all(keep, send):
    v = keep + partner(send, "core", 1).astype(f32)
    for step, field, dtype in PLAN:
        v = step(v, field, dtype)
    return v.astype(f32)


def dft_parts(size):
    index = np.arange(size)
    phase = (index[:, None] * index[None, :]) % size
    angle = 2.0 * np.pi / size * phase
    cosine = (np.cos(angle) / np.sqrt(size)).astype(jnp.bfloat16).astype(np.float32)
    sine = (np.sin(angle) / np.sqrt(size)).astype(jnp.bfloat16).astype(np.float32)
    return cosine, sine


def tables(size):
    half = size // 2
    c, s = dft_parts(size)
    order = np.concatenate([np.arange(0, size, 2), np.arange(1, size, 2)])
    fc, fs = c[order], s[order]
    left = np.block([[fc, fs], [-fs, fc]])
    cols = []
    for q in range(2):
        pick = order[q * half : (q + 1) * half]
        cols.append(np.block([[c[:, pick], -s[:, pick]], [s[:, pick], c[:, pick]]]))
    right = np.concatenate(cols, 1)
    gl, gr = [], []
    for q in range(2):
        ce, se = c[:half, q::2], s[:half, q::2]
        gl.append(np.block([[ce, -se], [se, ce]]))
        cr, sr = c[q::2, :half], s[q::2, :half]
        gr.append(np.block([[cr, sr], [-sr, cr]]))
    perm = np.zeros((size, size), np.float32)
    perm[np.arange(size), order] = 1.0
    to = lambda a: jnp.asarray(np.asarray(a, np.float32).astype(jnp.bfloat16))
    return to(left), to(right), to(np.stack(gl)), to(np.stack(gr)), to(perm), to(perm.T)


def prep_kernel(frames, rows, cols, out):
    def one(s, _):
        a = jnp.dot(rows[...], frames[s], preferred_element_type=f32).astype(bf16)
        out[s] = jnp.dot(a, cols[...], preferred_element_type=f32).astype(bf16)
        return 0

    lax.fori_loop(0, frames.shape[0], one, 0)


def choose(pos, cnt, wanted, todo, frames_hbm, frames, sem):
    todo[0] = 0

    def pick(s, k):
        take = wanted(pos[s, 1])

        @pl.when(take)
        def _():
            todo[k] = s
            pltpu.make_async_copy(frames_hbm.at[s], frames.at[s], sem.at[s]).start()

        return k + take.astype(jnp.int32)

    return lax.fori_loop(0, cnt[0], pick, 0)


def await_frames(count, todo, frames_hbm, frames, sem):
    def one(k, _):
        s = todo[k]
        pltpu.make_async_copy(frames_hbm.at[s], frames.at[s], sem.at[s]).wait()
        return 0

    lax.fori_loop(0, count, one, 0)


def positions_pass(
    pos, count, base, blocks, clear, probe, frames, tables, p_out,
    ext, gext, pat, xs, hs, sp, ws, ib, hb, eb, todo,
):
    left, right, gl, gr = tables
    n = probe.shape[-1]
    h = n // 2
    ch = 16
    last = jnp.maximum(count - 1, 0)

    def window(t):
        s = todo[jnp.clip(t, 0, last)]
        c = pos[s, 1]
        sh = lax.rem(c, 128)
        cb = jnp.clip(c // 128 - base, 0, blocks - 3)
        return s, pos[s, 0], cb, sh, lax.rem(384 - sh, 384)

    def patch_rows(win, i, ch=16):
        _, r, cb, _, unshift = win
        out = []
        for p in range(2):
            w = jnp.concatenate([ext[p, cb + b, pl.ds(r + i, ch), :] for b in range(3)], 1)
            out.append(pltpu.roll(w, unshift, 1)[:, :n])
        return out

    def wave_rows(win, slot, i):
        o = patch_rows(win, i)
        for p in range(2):
            pat[slot, p, i : i + ch, :] = o[p]
        for m in range(2):
            pr = probe[m, 0, i : i + ch, :]
            pi = probe[m, 1, i : i + ch, :]
            xs[m, i : i + ch, :] = (pr * o[0] - pi * o[1]).astype(bf16)
            xs[m, n + i : n + i + ch, :] = (pr * o[1] + pi * o[0]).astype(bf16)

    def forward_left(m, part):
        half = jnp.dot(left[part * n : (part + 1) * n, :], xs[m], preferred_element_type=f32)
        hs[m, :, part * n : (part + 1) * n] = half.astype(bf16)

    def forward_right(m, q):
        sp[m, q] = jnp.dot(hs[m], right[:, q * n : (q + 1) * n], preferred_element_type=f32)

    def weigh_rows(win, q, i):
        s = win[0]
        rows = i % h
        par = i // h
        v = [sp[m, q, i : i + ch, :] for m in range(2)]
        e = v[0] * v[0] + v[1] * v[1]
        inten = e[:, :h] + e[:, h:] + 1.0
        f = 1.0 - frames[s, i : i + ch, q * h : (q + 1) * h].astype(f32) * lax.rsqrt(inten)
        for m in range(2):
            for part in range(2):
                ws[m, par, part * h + rows : part * h + rows + ch, q * h : (q + 1) * h] = (
                    v[m][:, part * h : (part + 1) * h] * f
                ).astype(bf16)

    def inverse_left(m, par):
        ib[m, par] = jnp.dot(gl[par], ws[m, par], preferred_element_type=f32)

    def join_rows(m, part, i):
        a = ib[m, 0, part * h + i : part * h + i + ch, :]
        b = ib[m, 1, part * h + i : part * h + i + ch, :]
        up = (a + b).astype(bf16)
        dn = (a - b).astype(bf16)
        for q in range(2):
            hb[m, q, i : i + ch, part * h : (part + 1) * h] = up[:, q * h : (q + 1) * h]
            hb[m, q, h + i : h + i + ch, part * h : (part + 1) * h] = dn[:, q * h : (q + 1) * h]

    def inverse_right(m, q):
        eb[m, q] = jnp.dot(hb[m, q], gr[q], preferred_element_type=f32)

    def add_rows(win, slot, i0):
        for i in range(i0, i0 + ch, 8):
            add_some(win, slot, i)

    def add_some(win, slot, i):
        _, r, cb, sh, _ = win
        ore = pat[slot, 0, i : i + 8, :]
        oim = pat[slot, 1, i : i + 8, :]
        acc = None
        for m in range(2):
            e = eb[m, 0, i : i + 8, :]
            d = eb[m, 1, i : i + 8, :]
            up = e + d
            dn = e - d
            bre = jnp.concatenate([up[:, :h], dn[:, :h]], 1)
            bim = jnp.concatenate([up[:, h:], dn[:, h:]], 1)
            pr = probe[m, 0, i : i + 8, :]
            pi = probe[m, 1, i : i + 8, :]
            g = (pr * bre + pi * bim, pr * bim - pi * bre)
            acc = g if m == 0 else (acc[0] + g[0], acc[1] + g[1])
            p_out[m, 0, i : i + 8, :] += ore * bre + oim * bim
            p_out[m, 1, i : i + 8, :] += ore * bim - oim * bre
        zero = jnp.zeros((8, 128), f32)
        v = [pltpu.roll(jnp.concatenate([x, zero], 1), sh, 1) for x in acc]
        new = [
            gext[p, cb + b, pl.ds(r + i, 8), :] + v[p][:, b * 128 : (b + 1) * 128]
            for p in range(2)
            for b in range(3)
        ]
        for p in range(2):
            for b in range(3):
                gext[p, cb + b, pl.ds(r + i, 8), :] = new[p * 3 + b]

    chunks = list(range(0, n, ch))
    pairs = [(m, k) for m in range(2) for k in range(2)]

    def front(t):
        now = window(t)
        slot = lax.rem(t, 2)
        for i in chunks:
            wave_rows(now, slot, i)
        for m, part in pairs:
            forward_left(m, part)
        for q in range(2):
            for m in range(2):
                forward_right(m, q)
            for i in chunks:
                weigh_rows(now, q, i)

    def rear(t):
        old = window(t)
        slot = lax.rem(t, 2)
        for m in range(2):
            for par in range(2):
                inverse_left(m, par)
            for part in range(2):
                for i in range(0, h, ch):
                    join_rows(m, part, i)
            for q in range(2):
                inverse_right(m, q)
        for i in chunks:
            add_rows(old, slot, i)

    def both(t, _):
        now = window(t)
        old = window(t - 1)
        new_slot = lax.rem(t, 2)
        old_slot = 1 - new_slot
        for k, (m, par) in enumerate(pairs):
            inverse_left(m, par)
            for i in chunks[2 * k : 2 * k + 2]:
                wave_rows(now, new_slot, i)
        for m in range(2):
            for part in range(2):
                for i in range(0, h, ch):
                    join_rows(m, part, i)
        for k, (m, q) in enumerate(pairs):
            inverse_right(m, q)
            for i in chunks[8 + 2 * k : 8 + 2 * k + 2]:
                wave_rows(now, new_slot, i)
        for k, (m, part) in enumerate(pairs):
            forward_left(m, part)
            for i in chunks[3 * k : 3 * k + 3]:
                add_rows(old, old_slot, i)
        for m in range(2):
            forward_right(m, 0)
            for i in chunks[12 + 2 * m : 12 + 2 * m + 2]:
                add_rows(old, old_slot, i)
        for m in range(2):
            forward_right(m, 1)
            for i in chunks[8 * m : 8 * m + 8]:
                weigh_rows(now, 0, i)
        for i in chunks:
            weigh_rows(now, 1, i)
        return 0

    @pl.when(count > 0)
    def _():
        front(0)

    clear()
    lax.fori_loop(1, count, both, 0)

    @pl.when(count > 0)
    def _():
        rear(count - 1)


def fill(ext, sources):
    for p in range(2):
        for src, c_from, c_to, r0, c0 in sources:
            for b in range((c_to - c_from) // 128):
                lo = c_from + b * 128
                ext[p, c0 // 128 + b, r0 : r0 + src.shape[1], :] = src[p, :, lo : lo + 128].astype(f32)


def drain(gext, targets):
    for p in range(2):
        for dst, d0, width, r0, c0 in targets:
            for b in range(width // 128):
                dst[p, :, d0 + b * 128 : d0 + (b + 1) * 128] = gext[
                    p, c0 // 128 + b, r0 : r0 + dst.shape[1], :
                ].astype(dst.dtype)


def fetch(sources, targets, sems):
    copies = [pltpu.make_async_copy(s, d, sems.at[k]) for k, (s, d) in enumerate(zip(sources, targets))]
    for copy in copies:
        copy.start()
    return copies


def inner_kernel(
    pos, cnt, own_hbm, below_hbm, probe_hbm, frames_hbm, left_hbm, right_hbm, gl_hbm, gr_hbm,
    g_own, g_below, carry, p_out,
    own, below, probe, frames, left, right, gl, gr, sems, frame_sems, ext, gext, *scratch,
):
    copies = fetch(
        (own_hbm, below_hbm, probe_hbm, left_hbm, right_hbm, gl_hbm, gr_hbm),
        (own, below, probe, left, right, gl, gr),
        sems,
    )
    n = probe.shape[-1]
    tr, tc = own.shape[1:]
    inner = tc - n
    todo = scratch[-1]
    count = choose(pos, cnt, lambda c: c < inner, todo, frames_hbm, frames, frame_sems)
    copies[0].wait()
    fill(ext, ((own, 0, tc, 0, 0),))
    copies[1].wait()
    fill(ext, ((below, 0, tc, tr, 0),))
    for copy in copies[2:]:
        copy.wait()
    await_frames(count, todo, frames_hbm, frames, frame_sems)

    def clear():
        gext[...] = jnp.zeros_like(gext)
        p_out[...] = jnp.zeros_like(p_out)

    positions_pass(
        pos, count, 0, tc // 128, clear, probe, frames, (left, right, gl, gr), p_out,
        ext, gext, *scratch,
    )
    drain(gext, ((g_own, 0, inner, 0, 0), (g_below, 0, inner, tr, 0)))
    for p in range(2):
        for b in range(n // 128):
            carry[p, b] = gext[p, inner // 128 + b]


def edge_kernel(
    scale, pos, cnt, core, own_hbm, below_hbm, strip_hbm, corner_hbm, carry_hbm, p_hbm, probe_hbm, frames_hbm,
    left_hbm, right_hbm, gl_hbm, gr_hbm,
    g_own, g_rows, g_strip, p_keep, p_send,
    own, below, strip, corner, carry, p_in, probe, frames, left, right, gl, gr, sems, frame_sems, p_out, ext, gext, *scratch,
):
    n = probe.shape[-1]
    tr, tc = own_hbm.shape[1:]
    inner = tc - n
    copies = fetch(
        (
            own_hbm.at[:, :, inner:tc], below_hbm.at[:, :, inner:tc], strip_hbm, corner_hbm, probe_hbm,
            left_hbm, right_hbm, gl_hbm, gr_hbm, p_hbm, carry_hbm,
        ),
        (own, below, strip, corner, probe, left, right, gl, gr, p_in, carry),
        sems,
    )
    todo = scratch[-1]
    count = choose(pos, cnt, lambda c: c >= inner, todo, frames_hbm, frames, frame_sems)
    for copy in copies[:4]:
        copy.wait()
    fill(ext, ((own, 0, n, 0, 0), (below, 0, n, tr, 0), (strip, 0, n, 0, n), (corner, 0, n, tr, n)))
    for copy in copies[4:9]:
        copy.wait()
    await_frames(count, todo, frames_hbm, frames, frame_sems)

    def clear():
        for copy in copies[9:]:
            copy.wait()
        p_out[...] = p_in[...]
        for p in range(2):
            for b in range(n // 128):
                gext[p, b] = carry[p, b]
                gext[p, n // 128 + b] = jnp.zeros_like(gext[p, b])

    positions_pass(
        pos, count, inner // 128, 2 * n // 128, clear, probe, frames,
        (left, right, gl, gr), p_out, ext, gext, *scratch,
    )
    p_keep[...] = p_out[core[0]] * scale
    p_send[...] = (p_out[1 - core[0]] * scale).astype(bf16)
    drain(gext, ((g_own, 0, n, 0, 0), (g_rows, 0, 2 * n, tr, 0), (g_strip, 0, n, 0, n)))


def body(object_field, probe, measured, positions, counts):
    size = probe.shape[-1]
    tile_rows, tile_cols = object_field.shape[1:]
    slots = measured.shape[2]
    left, right, gl, gr, perm, perm_t = tables(size)
    vmem = pl.BlockSpec(memory_space=pltpu.VMEM)
    stay = pl.BlockSpec(memory_space=pl.ANY)
    smem = pl.BlockSpec(memory_space=pltpu.SMEM)
    pos, cnt = positions[0, 0], counts[0]
    core = (lax.axis_index("row") & 1).astype(jnp.int32).reshape(1)
    inner = tile_cols - size
    rows = tile_rows + size

    below = shifted(object_field, "row", -1)
    strip = shifted(object_field[:, :, :size], "col", -1)
    corner = shifted(strip, "row", -1)
    frames = pl.pallas_call(
        prep_kernel,
        out_shape=jax.ShapeDtypeStruct(measured.shape[2:], bf16),
        in_specs=[vmem] * 3,
        out_specs=vmem,
        compiler_params=pltpu.CompilerParams(vmem_limit_bytes=8 * 2**20),
        cost_estimate=pl.CostEstimate(
            flops=slots * 4 * size**3, bytes_accessed=4 * slots * size * size, transcendentals=0
        ),
    )(measured[0, 0], perm, perm_t)

    def scratch(blocks):
        return [
            pltpu.VMEM((2, blocks, rows, 128), f32),
            pltpu.VMEM((2, blocks, rows, 128), f32),
            pltpu.VMEM((2, 2, size, size), f32),
            pltpu.VMEM((2, 2 * size, size), bf16),
            pltpu.VMEM((2, size, 2 * size), bf16),
            pltpu.VMEM((2, 2, size, size), f32),
            pltpu.VMEM((2, 2, size, size), bf16),
            pltpu.VMEM((2, 2, size, size), f32),
            pltpu.VMEM((2, 2, size, size), bf16),
            pltpu.VMEM((2, 2, size, size), f32),
            pltpu.SMEM((slots,), jnp.int32),
        ]

    fixed = [pltpu.VMEM(x.shape, x.dtype) for x in (probe, frames, left, right, gl, gr)]
    params = pltpu.CompilerParams(
        vmem_limit_bytes=60 * 2**20
    )
    g_main, g_band, carry, p_part = pl.pallas_call(
        inner_kernel,
        out_shape=(
            jax.ShapeDtypeStruct((2, tile_rows, inner), f32),
            jax.ShapeDtypeStruct((2, size, inner), bf16),
            jax.ShapeDtypeStruct((2, size // 128, rows, 128), f32),
            jax.ShapeDtypeStruct(probe.shape, f32),
        ),
        in_specs=[smem, smem] + [stay] * 8,
        out_specs=[vmem] * 4,
        scratch_shapes=[
            pltpu.VMEM((2, tile_rows, tile_cols), bf16),
            pltpu.VMEM((2, size, tile_cols), bf16),
        ]
        + fixed
        + [pltpu.SemaphoreType.DMA((7,)), pltpu.SemaphoreType.DMA((slots,))]
        + scratch(tile_cols // 128),
        compiler_params=params,
        cost_estimate=pl.CostEstimate(flops=9 * 2**30, bytes_accessed=12 * 2**20, transcendentals=0),
    )(pos, cnt, object_field, below, probe, frames, left, right, gl, gr)
    total = slots * lax.axis_size("row") * lax.axis_size("col")
    scale = 1.0 / math.sqrt(total)
    g_right, g_rows, g_strip, p_keep, p_send = pl.pallas_call(
        lambda *refs: edge_kernel(scale, *refs),
        out_shape=(
            jax.ShapeDtypeStruct((2, tile_rows, size), f32),
            jax.ShapeDtypeStruct((2, size, 2 * size), bf16),
            jax.ShapeDtypeStruct((2, tile_rows, size), bf16),
            jax.ShapeDtypeStruct(probe.shape[1:], f32),
            jax.ShapeDtypeStruct(probe.shape[1:], bf16),
        ),
        in_specs=[smem] * 3 + [stay] * 12,
        out_specs=[vmem] * 5,
        scratch_shapes=[
            pltpu.VMEM((2, tile_rows, size), bf16),
            pltpu.VMEM((2, size, size), bf16),
            pltpu.VMEM((2, tile_rows, size), bf16),
            pltpu.VMEM((2, size, size), bf16),
            pltpu.VMEM((2, size // 128, rows, 128), f32),
            pltpu.VMEM(probe.shape, f32),
        ]
        + fixed
        + [pltpu.SemaphoreType.DMA((11,)), pltpu.SemaphoreType.DMA((slots,)), pltpu.VMEM(probe.shape, f32)]
        + scratch(2 * size // 128),
        compiler_params=params,
        cost_estimate=pl.CostEstimate(flops=3 * 2**30, bytes_accessed=12 * 2**20, transcendentals=0),
    )(pos, cnt, core, object_field, below, strip, corner, carry, p_part, probe, frames, left, right, gl, gr)

    band = shifted(g_band, "row", 1)
    tail = shifted(g_rows, "row", 1)
    to_right = (g_strip.astype(f32) + tail[:, :, size:].astype(f32)).astype(bf16)
    side = shifted(to_right, "col", 1)
    probe_grad = reduce_all(p_keep.reshape(-1, size), p_send.reshape(-1, size)).reshape(probe.shape)
    object_grad = jnp.concatenate(
        [g_main + band.astype(f32), g_right + tail[:, :, :size].astype(f32)], 2
    )
    object_grad = object_grad.at[:, :, :size].add(side.astype(f32))
    return (object_grad, probe_grad)


def solution(mesh):
    placed = (
        P(None, "row", "col"),
        P(),
        P("row", "col", None, None, None),
        P("row", "col", None, None),
        P("row", "col"),
    )
    return jax.shard_map(
        body, mesh=mesh, in_specs=placed, out_specs=(P(None, "row", "col"), P()), check_vma=False
    )
```

```python
import math

import jax
import jax.numpy as jnp
import numpy as np
from jax import lax
from jax.experimental import pallas as pl
from jax.experimental.pallas import tpu as pltpu
from jax.sharding import PartitionSpec as P


f32 = jnp.float32
bf16 = jnp.bfloat16


def shifted(x, axis, by):
    peers = lax.axis_size(axis)
    pairs = [(i, i + by) for i in range(peers) if 0 <= i + by < peers]
    return lax.ppermute(x, axis, pairs)


Y = [(8, 0), (16, 0), (24, 0)]
X = [(0, 2), (0, 4), (0, 6)]
FIELDS = {
    "core": ([(1, 0)], [(1, 0)]),
    "first": (Y, X),
    "second": (X, Y),
    "z0": ([(2, 0)], [(2, 0)]),
    "z1": ([(4, 0)], [(4, 0)]),
    "z2": ([(4, 1)], [(4, 1)]),
}


def partner(v, field, d):
    masks = [masks[d - 1] for masks in FIELDS[field]]
    rows, cols = lax.axis_size("row"), lax.axis_size("col")
    pairs = []
    for r in range(rows):
        for c in range(cols):
            row, col = masks[r & 1]
            pairs.append((r * cols + c, (r ^ row) * cols + (c ^ col)))
    return lax.ppermute(v, ("row", "col"), pairs)


def members(field):
    return len(FIELDS[field][0]) + 1


def place(field):
    if field == "core":
        return lax.axis_index("row") & 1
    return jnp.where(lax.axis_index("row") & 1 == 0, lax.axis_index("row") >> 3, lax.axis_index("col") >> 1)


def scatter_sum(v, field, dtype):
    n = members(field)
    g = place(field)
    k = v.shape[0] // n
    total = lax.dynamic_slice_in_dim(v, g * k, k, 0)
    got = [
        partner(lax.dynamic_slice_in_dim(v, (g ^ d) * k, k, 0).astype(dtype), field, d)
        for d in range(1, n)
    ]
    for part in got:
        total = total + part.astype(f32)
    return total


def full_sum(v, field, dtype):
    n = members(field)
    sent = v.astype(dtype)
    parts = [sent.astype(f32)] + [partner(sent, field, d).astype(f32) for d in range(1, n)]
    while len(parts) > 1:
        parts = [parts[i] + parts[i + 1] for i in range(0, len(parts), 2)]
    return parts[0]


def gather(v, field, dtype):
    n = members(field)
    g = place(field)
    k = v.shape[0]
    sent = v.astype(dtype)
    got = [partner(sent, field, d) for d in range(1, n)]
    out = jnp.zeros((n * k,) + v.shape[1:], dtype)
    out = lax.dynamic_update_slice_in_dim(out, sent, g * k, 0)
    for d in range(1, n):
        out = lax.dynamic_update_slice_in_dim(out, got[d - 1], (g ^ d) * k, 0)
    return out


PLAN = (
    (scatter_sum, "first", bf16),
    (full_sum, "z0", bf16),
    (full_sum, "z1", bf16),
    (full_sum, "z2", bf16),
    (full_sum, "second", bf16),
    (gather, "first", bf16),
    (gather, "core", bf16),
)


def reduce_all(keep, send):
    v = keep + partner(send, "core", 1).astype(f32)
    for step, field, dtype in PLAN:
        v = step(v, field, dtype)
    return v.astype(f32)


def dft_parts(size):
    index = np.arange(size)
    phase = (index[:, None] * index[None, :]) % size
    angle = 2.0 * np.pi / size * phase
    cosine = (np.cos(angle) / np.sqrt(size)).astype(jnp.bfloat16).astype(np.float32)
    sine = (np.sin(angle) / np.sqrt(size)).astype(jnp.bfloat16).astype(np.float32)
    return cosine, sine


def tables(size):
    half = size // 2
    c, s = dft_parts(size)
    order = np.concatenate([np.arange(0, size, 2), np.arange(1, size, 2)])
    fc, fs = c[order], s[order]
    left = np.block([[fc, fs], [-fs, fc]])
    cols = []
    for q in range(2):
        pick = order[q * half : (q + 1) * half]
        cols.append(np.block([[c[:, pick], -s[:, pick]], [s[:, pick], c[:, pick]]]))
    right = np.concatenate(cols, 1)
    gl, gr = [], []
    for q in range(2):
        ce, se = c[:half, q::2], s[:half, q::2]
        gl.append(np.block([[ce, -se], [se, ce]]))
        cr, sr = c[q::2, :half], s[q::2, :half]
        gr.append(np.block([[cr, sr], [-sr, cr]]))
    perm = np.zeros((size, size), np.float32)
    perm[np.arange(size), order] = 1.0
    to = lambda a: jnp.asarray(np.asarray(a, np.float32).astype(jnp.bfloat16))
    return to(left), to(right), to(np.stack(gl)), to(np.stack(gr)), to(perm), to(perm.T)


def prep_kernel(frames, rows, cols, out):
    def one(s, _):
        a = jnp.dot(rows[...], frames[s], preferred_element_type=f32).astype(bf16)
        out[s] = jnp.dot(a, cols[...], preferred_element_type=f32).astype(bf16)
        return 0

    lax.fori_loop(0, frames.shape[0], one, 0)


def choose(pos, cnt, wanted, todo, frames_hbm, frames, sem):
    todo[0] = 0

    def pick(s, k):
        take = wanted(pos[s, 1])

        @pl.when(take)
        def _():
            todo[k] = s
            pltpu.make_async_copy(frames_hbm.at[s], frames.at[s], sem.at[s]).start()

        return k + take.astype(jnp.int32)

    return lax.fori_loop(0, cnt[0], pick, 0)


def await_frames(count, todo, frames_hbm, frames, sem):
    def one(k, _):
        s = todo[k]
        pltpu.make_async_copy(frames_hbm.at[s], frames.at[s], sem.at[s]).wait()
        return 0

    lax.fori_loop(0, count, one, 0)


def positions_pass(
    pos, count, base, blocks, clear, probe, frames, tables, p_out,
    ext, gext, pat, xs, hs, sp, ws, ib, hb, eb, todo,
):
    left, right, gl, gr = tables
    n = probe.shape[-1]
    h = n // 2
    ch = 16
    last = jnp.maximum(count - 1, 0)

    def window(t):
        s = todo[jnp.clip(t, 0, last)]
        c = pos[s, 1]
        sh = lax.rem(c, 128)
        cb = jnp.clip(c // 128 - base, 0, blocks - 3)
        return s, pos[s, 0], cb, sh, lax.rem(384 - sh, 384)

    def patch_rows(win, i, ch=16):
        _, r, cb, _, unshift = win
        out = []
        for p in range(2):
            w = jnp.concatenate([ext[p, cb + b, pl.ds(r + i, ch), :] for b in range(3)], 1)
            out.append(pltpu.roll(w, unshift, 1)[:, :n])
        return out

    def wave_rows(win, slot, i):
        o = patch_rows(win, i)
        for p in range(2):
            pat[slot, p, i : i + ch, :] = o[p]
        for m in range(2):
            pr = probe[m, 0, i : i + ch, :]
            pi = probe[m, 1, i : i + ch, :]
            xs[m, i : i + ch, :] = (pr * o[0] - pi * o[1]).astype(bf16)
            xs[m, n + i : n + i + ch, :] = (pr * o[1] + pi * o[0]).astype(bf16)

    def forward_left(m, part):
        half = jnp.dot(left[part * n : (part + 1) * n, :], xs[m], preferred_element_type=f32)
        hs[m, :, part * n : (part + 1) * n] = half.astype(bf16)

    def forward_right(m, q):
        sp[m, q] = jnp.dot(hs[m], right[:, q * n : (q + 1) * n], preferred_element_type=f32)

    def weigh_rows(win, q, i):
        s = win[0]
        rows = i % h
        par = i // h
        v = [sp[m, q, i : i + ch, :] for m in range(2)]
        e = v[0] * v[0] + v[1] * v[1]
        inten = e[:, :h] + e[:, h:] + 1.0
        f = 1.0 - frames[s, i : i + ch, q * h : (q + 1) * h].astype(f32) * lax.rsqrt(inten)
        for m in range(2):
            for part in range(2):
                ws[m, par, part * h + rows : part * h + rows + ch, q * h : (q + 1) * h] = (
                    v[m][:, part * h : (part + 1) * h] * f
                ).astype(bf16)

    def inverse_left(m, par):
        ib[m, par] = jnp.dot(gl[par], ws[m, par], preferred_element_type=f32)

    def join_rows(m, part, i):
        a = ib[m, 0, part * h + i : part * h + i + ch, :]
        b = ib[m, 1, part * h + i : part * h + i + ch, :]
        up = (a + b).astype(bf16)
        dn = (a - b).astype(bf16)
        for q in range(2):
            hb[m, q, i : i + ch, part * h : (part + 1) * h] = up[:, q * h : (q + 1) * h]
            hb[m, q, h + i : h + i + ch, part * h : (part + 1) * h] = dn[:, q * h : (q + 1) * h]

    def inverse_right(m, q):
        eb[m, q] = jnp.dot(hb[m, q], gr[q], preferred_element_type=f32)

    def add_rows(win, slot, i0):
        for i in range(i0, i0 + ch, 8):
            add_some(win, slot, i)

    def add_some(win, slot, i):
        _, r, cb, sh, _ = win
        ore = pat[slot, 0, i : i + 8, :]
        oim = pat[slot, 1, i : i + 8, :]
        acc = None
        for m in range(2):
            e = eb[m, 0, i : i + 8, :]
            d = eb[m, 1, i : i + 8, :]
            up = e + d
            dn = e - d
            bre = jnp.concatenate([up[:, :h], dn[:, :h]], 1)
            bim = jnp.concatenate([up[:, h:], dn[:, h:]], 1)
            pr = probe[m, 0, i : i + 8, :]
            pi = probe[m, 1, i : i + 8, :]
            g = (pr * bre + pi * bim, pr * bim - pi * bre)
            acc = g if m == 0 else (acc[0] + g[0], acc[1] + g[1])
            p_out[m, 0, i : i + 8, :] += ore * bre + oim * bim
            p_out[m, 1, i : i + 8, :] += ore * bim - oim * bre
        zero = jnp.zeros((8, 128), f32)
        v = [pltpu.roll(jnp.concatenate([x, zero], 1), sh, 1) for x in acc]
        new = [
            gext[p, cb + b, pl.ds(r + i, 8), :] + v[p][:, b * 128 : (b + 1) * 128]
            for p in range(2)
            for b in range(3)
        ]
        for p in range(2):
            for b in range(3):
                gext[p, cb + b, pl.ds(r + i, 8), :] = new[p * 3 + b]

    chunks = list(range(0, n, ch))
    pairs = [(m, k) for m in range(2) for k in range(2)]

    def front(t):
        now = window(t)
        slot = lax.rem(t, 2)
        for i in chunks:
            wave_rows(now, slot, i)
        for m, part in pairs:
            forward_left(m, part)
        for q in range(2):
            for m in range(2):
                forward_right(m, q)
            for i in chunks:
                weigh_rows(now, q, i)

    def rear(t):
        old = window(t)
        slot = lax.rem(t, 2)
        for m in range(2):
            for par in range(2):
                inverse_left(m, par)
            for part in range(2):
                for i in range(0, h, ch):
                    join_rows(m, part, i)
            for q in range(2):
                inverse_right(m, q)
        for i in chunks:
            add_rows(old, slot, i)

    def both(t, _):
        now = window(t)
        old = window(t - 1)
        new_slot = lax.rem(t, 2)
        old_slot = 1 - new_slot
        for k, (m, par) in enumerate(pairs):
            inverse_left(m, par)
            for i in chunks[2 * k : 2 * k + 2]:
                wave_rows(now, new_slot, i)
        for m in range(2):
            for part in range(2):
                for i in range(0, h, ch):
                    join_rows(m, part, i)
        for k, (m, q) in enumerate(pairs):
            inverse_right(m, q)
            for i in chunks[8 + 2 * k : 8 + 2 * k + 2]:
                wave_rows(now, new_slot, i)
        for k, (m, part) in enumerate(pairs):
            forward_left(m, part)
            for i in chunks[3 * k : 3 * k + 3]:
                add_rows(old, old_slot, i)
        for m in range(2):
            forward_right(m, 0)
            for i in chunks[12 + 2 * m : 12 + 2 * m + 2]:
                add_rows(old, old_slot, i)
        for m in range(2):
            forward_right(m, 1)
            for i in chunks[8 * m : 8 * m + 8]:
                weigh_rows(now, 0, i)
        for i in chunks:
            weigh_rows(now, 1, i)
        return 0

    @pl.when(count > 0)
    def _():
        front(0)

    clear()
    lax.fori_loop(1, count, both, 0)

    @pl.when(count > 0)
    def _():
        rear(count - 1)


def fill(ext, sources):
    for p in range(2):
        for src, c_from, c_to, r0, c0 in sources:
            for b in range((c_to - c_from) // 128):
                lo = c_from + b * 128
                ext[p, c0 // 128 + b, r0 : r0 + src.shape[1], :] = src[p, :, lo : lo + 128].astype(f32)


def drain(gext, targets):
    for p in range(2):
        for dst, d0, width, r0, c0 in targets:
            for b in range(width // 128):
                dst[p, :, d0 + b * 128 : d0 + (b + 1) * 128] = gext[
                    p, c0 // 128 + b, r0 : r0 + dst.shape[1], :
                ].astype(dst.dtype)


def fetch(sources, targets, sems):
    copies = [pltpu.make_async_copy(s, d, sems.at[k]) for k, (s, d) in enumerate(zip(sources, targets))]
    for copy in copies:
        copy.start()
    return copies


def send_out(source, target, sem):
    copy = pltpu.make_async_copy(source, target, sem)
    copy.start()
    return copy


def inner_kernel(
    pos, cnt, own_hbm, below_hbm, probe_hbm, frames_hbm, left_hbm, right_hbm, gl_hbm, gr_hbm,
    g_own_hbm, g_below_hbm, carry_hbm, p_hbm,
    own, below, probe, frames, left, right, gl, gr, sems, frame_sems, out_sems, g_own, g_below, p_out,
    ext, gext, *scratch,
):
    copies = fetch(
        (own_hbm, below_hbm, probe_hbm, left_hbm, right_hbm, gl_hbm, gr_hbm),
        (own, below, probe, left, right, gl, gr),
        sems,
    )
    n = probe.shape[-1]
    tr, tc = own.shape[1:]
    inner = tc - n
    todo = scratch[-1]
    count = choose(pos, cnt, lambda c: c < inner, todo, frames_hbm, frames, frame_sems)
    copies[0].wait()
    fill(ext, ((own, 0, tc, 0, 0),))
    copies[1].wait()
    fill(ext, ((below, 0, tc, tr, 0),))
    for copy in copies[2:]:
        copy.wait()
    await_frames(count, todo, frames_hbm, frames, frame_sems)

    def clear():
        gext[...] = jnp.zeros_like(gext)
        p_out[...] = jnp.zeros_like(p_out)

    positions_pass(
        pos, count, 0, tc // 128, clear, probe, frames, (left, right, gl, gr), p_out,
        ext, gext, *scratch,
    )
    done = [send_out(p_out, p_hbm, out_sems.at[0])]
    for p in range(2):
        done.append(send_out(gext.at[p, pl.ds(inner // 128, n // 128)], carry_hbm.at[p], out_sems.at[1 + p]))
    drain(gext, ((g_below, 0, inner, tr, 0),))
    done.append(send_out(g_below, g_below_hbm, out_sems.at[3]))
    drain(gext, ((g_own, 0, inner, 0, 0),))
    done.append(send_out(g_own, g_own_hbm, out_sems.at[4]))
    for copy in done:
        copy.wait()


def edge_kernel(
    scale, pos, cnt, core, own_hbm, below_hbm, strip_hbm, corner_hbm, carry_hbm, p_hbm, probe_hbm, frames_hbm,
    left_hbm, right_hbm, gl_hbm, gr_hbm,
    g_own_hbm, g_rows_hbm, g_strip_hbm, p_keep_hbm, p_send_hbm,
    own, below, strip, corner, carry, p_in, probe, frames, left, right, gl, gr, sems, frame_sems, out_sems,
    g_own, g_rows, g_strip, p_keep, p_send, p_out, ext, gext, *scratch,
):
    n = probe.shape[-1]
    tr, tc = own_hbm.shape[1:]
    inner = tc - n
    copies = fetch(
        (
            own_hbm.at[:, :, inner:tc], below_hbm.at[:, :, inner:tc], strip_hbm, corner_hbm, probe_hbm,
            left_hbm, right_hbm, gl_hbm, gr_hbm, p_hbm, carry_hbm,
        ),
        (own, below, strip, corner, probe, left, right, gl, gr, p_in, carry),
        sems,
    )
    todo = scratch[-1]
    count = choose(pos, cnt, lambda c: c >= inner, todo, frames_hbm, frames, frame_sems)
    for copy in copies[:4]:
        copy.wait()
    fill(ext, ((own, 0, n, 0, 0), (below, 0, n, tr, 0), (strip, 0, n, 0, n), (corner, 0, n, tr, n)))
    for copy in copies[4:9]:
        copy.wait()
    await_frames(count, todo, frames_hbm, frames, frame_sems)

    def clear():
        for copy in copies[9:]:
            copy.wait()
        p_out[...] = p_in[...]
        for p in range(2):
            for b in range(n // 128):
                gext[p, b] = carry[p, b]
                gext[p, n // 128 + b] = jnp.zeros_like(gext[p, b])

    positions_pass(
        pos, count, inner // 128, 2 * n // 128, clear, probe, frames,
        (left, right, gl, gr), p_out, ext, gext, *scratch,
    )
    p_send[...] = (p_out[1 - core[0]] * scale).astype(bf16)
    done = [send_out(p_send, p_send_hbm, out_sems.at[0])]
    p_keep[...] = p_out[core[0]] * scale
    done.append(send_out(p_keep, p_keep_hbm, out_sems.at[1]))
    drain(gext, ((g_rows, 0, 2 * n, tr, 0),))
    done.append(send_out(g_rows, g_rows_hbm, out_sems.at[2]))
    drain(gext, ((g_strip, 0, n, 0, n),))
    done.append(send_out(g_strip, g_strip_hbm, out_sems.at[3]))
    drain(gext, ((g_own, 0, n, 0, 0),))
    done.append(send_out(g_own, g_own_hbm, out_sems.at[4]))
    for copy in done:
        copy.wait()


def body(object_field, probe, measured, positions, counts):
    size = probe.shape[-1]
    tile_rows, tile_cols = object_field.shape[1:]
    slots = measured.shape[2]
    left, right, gl, gr, perm, perm_t = tables(size)
    vmem = pl.BlockSpec(memory_space=pltpu.VMEM)
    stay = pl.BlockSpec(memory_space=pl.ANY)
    smem = pl.BlockSpec(memory_space=pltpu.SMEM)
    pos, cnt = positions[0, 0], counts[0]
    core = (lax.axis_index("row") & 1).astype(jnp.int32).reshape(1)
    inner = tile_cols - size
    rows = tile_rows + size

    below = shifted(object_field, "row", -1)
    strip = shifted(object_field[:, :, :size], "col", -1)
    corner = shifted(strip, "row", -1)
    frames = pl.pallas_call(
        prep_kernel,
        out_shape=jax.ShapeDtypeStruct(measured.shape[2:], bf16),
        in_specs=[vmem] * 3,
        out_specs=vmem,
        compiler_params=pltpu.CompilerParams(vmem_limit_bytes=8 * 2**20),
        cost_estimate=pl.CostEstimate(
            flops=slots * 4 * size**3, bytes_accessed=4 * slots * size * size, transcendentals=0
        ),
    )(measured[0, 0], perm, perm_t)

    def scratch(blocks):
        return [
            pltpu.VMEM((2, blocks, rows, 128), f32),
            pltpu.VMEM((2, blocks, rows, 128), f32),
            pltpu.VMEM((2, 2, size, size), f32),
            pltpu.VMEM((2, 2 * size, size), bf16),
            pltpu.VMEM((2, size, 2 * size), bf16),
            pltpu.VMEM((2, 2, size, size), f32),
            pltpu.VMEM((2, 2, size, size), bf16),
            pltpu.VMEM((2, 2, size, size), f32),
            pltpu.VMEM((2, 2, size, size), bf16),
            pltpu.VMEM((2, 2, size, size), f32),
            pltpu.SMEM((slots,), jnp.int32),
        ]

    fixed = [pltpu.VMEM(x.shape, x.dtype) for x in (probe, frames, left, right, gl, gr)]
    params = pltpu.CompilerParams(
        vmem_limit_bytes=60 * 2**20
    )
    g_main, g_band, carry, p_part = pl.pallas_call(
        inner_kernel,
        out_shape=(
            jax.ShapeDtypeStruct((2, tile_rows, inner), f32),
            jax.ShapeDtypeStruct((2, size, inner), bf16),
            jax.ShapeDtypeStruct((2, size // 128, rows, 128), f32),
            jax.ShapeDtypeStruct(probe.shape, f32),
        ),
        in_specs=[smem, smem] + [stay] * 8,
        out_specs=[stay] * 4,
        scratch_shapes=[
            pltpu.VMEM((2, tile_rows, tile_cols), bf16),
            pltpu.VMEM((2, size, tile_cols), bf16),
        ]
        + fixed
        + [pltpu.SemaphoreType.DMA((k,)) for k in (7, slots, 5)]
        + [
            pltpu.VMEM((2, tile_rows, inner), f32),
            pltpu.VMEM((2, size, inner), bf16),
            pltpu.VMEM(probe.shape, f32),
        ]
        + scratch(tile_cols // 128),
        compiler_params=params,
        cost_estimate=pl.CostEstimate(flops=9 * 2**30, bytes_accessed=12 * 2**20, transcendentals=0),
    )(pos, cnt, object_field, below, probe, frames, left, right, gl, gr)
    total = slots * lax.axis_size("row") * lax.axis_size("col")
    scale = 1.0 / math.sqrt(total)
    g_right, g_rows, g_strip, p_keep, p_send = pl.pallas_call(
        lambda *refs: edge_kernel(scale, *refs),
        out_shape=(
            jax.ShapeDtypeStruct((2, tile_rows, size), f32),
            jax.ShapeDtypeStruct((2, size, 2 * size), bf16),
            jax.ShapeDtypeStruct((2, tile_rows, size), bf16),
            jax.ShapeDtypeStruct(probe.shape[1:], f32),
            jax.ShapeDtypeStruct(probe.shape[1:], bf16),
        ),
        in_specs=[smem] * 3 + [stay] * 12,
        out_specs=[stay] * 5,
        scratch_shapes=[
            pltpu.VMEM((2, tile_rows, size), bf16),
            pltpu.VMEM((2, size, size), bf16),
            pltpu.VMEM((2, tile_rows, size), bf16),
            pltpu.VMEM((2, size, size), bf16),
            pltpu.VMEM((2, size // 128, rows, 128), f32),
            pltpu.VMEM(probe.shape, f32),
        ]
        + fixed
        + [pltpu.SemaphoreType.DMA((k,)) for k in (11, slots, 5)]
        + [
            pltpu.VMEM((2, tile_rows, size), f32),
            pltpu.VMEM((2, size, 2 * size), bf16),
            pltpu.VMEM((2, tile_rows, size), bf16),
            pltpu.VMEM(probe.shape[1:], f32),
            pltpu.VMEM(probe.shape[1:], bf16),
            pltpu.VMEM(probe.shape, f32),
        ]
        + scratch(2 * size // 128),
        compiler_params=params,
        cost_estimate=pl.CostEstimate(flops=3 * 2**30, bytes_accessed=12 * 2**20, transcendentals=0),
    )(pos, cnt, core, object_field, below, strip, corner, carry, p_part, probe, frames, left, right, gl, gr)

    band = shifted(g_band, "row", 1)
    tail = shifted(g_rows, "row", 1)
    to_right = (g_strip.astype(f32) + tail[:, :, size:].astype(f32)).astype(bf16)
    side = shifted(to_right, "col", 1)
    probe_grad = reduce_all(p_keep.reshape(-1, size), p_send.reshape(-1, size)).reshape(probe.shape)
    main = g_main + band.astype(f32)
    object_grad = jnp.concatenate(
        [main, g_right + tail[:, :, :size].astype(f32)], 2
    )
    object_grad = object_grad.at[:, :, :size].add(side.astype(f32))
    return (object_grad, probe_grad)


def solution(mesh):
    placed = (
        P(None, "row", "col"),
        P(),
        P("row", "col", None, None, None),
        P("row", "col", None, None),
        P("row", "col"),
    )
    return jax.shard_map(
        body, mesh=mesh, in_specs=placed, out_specs=(P(None, "row", "col"), P()), check_vma=False
    )
```

```python
import math

import jax
import jax.numpy as jnp
import numpy as np
from jax import lax
from jax.experimental import pallas as pl
from jax.experimental.pallas import tpu as pltpu
from jax.sharding import PartitionSpec as P


f32 = jnp.float32
bf16 = jnp.bfloat16


def shifted(x, axis, by):
    peers = lax.axis_size(axis)
    pairs = [(i, i + by) for i in range(peers) if 0 <= i + by < peers]
    return lax.ppermute(x, axis, pairs)


Y = [(8, 0), (16, 0), (24, 0)]
X = [(0, 2), (0, 4), (0, 6)]
FIELDS = {
    "core": ([(1, 0)], [(1, 0)]),
    "first": (Y, X),
    "second": (X, Y),
    "z0": ([(2, 0)], [(2, 0)]),
    "z1": ([(4, 0)], [(4, 0)]),
    "z2": ([(4, 1)], [(4, 1)]),
}


def partner(v, field, d):
    masks = [masks[d - 1] for masks in FIELDS[field]]
    rows, cols = lax.axis_size("row"), lax.axis_size("col")
    pairs = []
    for r in range(rows):
        for c in range(cols):
            row, col = masks[r & 1]
            pairs.append((r * cols + c, (r ^ row) * cols + (c ^ col)))
    return lax.ppermute(v, ("row", "col"), pairs)


def members(field):
    return len(FIELDS[field][0]) + 1


def place(field):
    if field == "core":
        return lax.axis_index("row") & 1
    return jnp.where(lax.axis_index("row") & 1 == 0, lax.axis_index("row") >> 3, lax.axis_index("col") >> 1)


def scatter_sum(v, field, dtype):
    n = members(field)
    g = place(field)
    k = v.shape[0] // n
    total = lax.dynamic_slice_in_dim(v, g * k, k, 0)
    got = [
        partner(lax.dynamic_slice_in_dim(v, (g ^ d) * k, k, 0).astype(dtype), field, d)
        for d in range(1, n)
    ]
    for part in got:
        total = total + part.astype(f32)
    return total


def full_sum(v, field, dtype):
    n = members(field)
    sent = v.astype(dtype)
    parts = [sent.astype(f32)] + [partner(sent, field, d).astype(f32) for d in range(1, n)]
    while len(parts) > 1:
        parts = [parts[i] + parts[i + 1] for i in range(0, len(parts), 2)]
    return parts[0]


def gather(v, field, dtype):
    n = members(field)
    g = place(field)
    k = v.shape[0]
    sent = v.astype(dtype)
    got = [partner(sent, field, d) for d in range(1, n)]
    out = jnp.zeros((n * k,) + v.shape[1:], dtype)
    out = lax.dynamic_update_slice_in_dim(out, sent, g * k, 0)
    for d in range(1, n):
        out = lax.dynamic_update_slice_in_dim(out, got[d - 1], (g ^ d) * k, 0)
    return out


PLAN = (
    (scatter_sum, "first", bf16),
    (full_sum, "z0", bf16),
    (full_sum, "z1", bf16),
    (full_sum, "z2", bf16),
    (full_sum, "second", bf16),
    (gather, "first", bf16),
    (gather, "core", bf16),
)


def reduce_all(keep, send):
    v = keep + partner(send, "core", 1).astype(f32)
    for step, field, dtype in PLAN:
        v = step(v, field, dtype)
    return v.astype(f32)


def dft_parts(size):
    index = np.arange(size)
    phase = (index[:, None] * index[None, :]) % size
    angle = 2.0 * np.pi / size * phase
    cosine = (np.cos(angle) / np.sqrt(size)).astype(jnp.bfloat16).astype(np.float32)
    sine = (np.sin(angle) / np.sqrt(size)).astype(jnp.bfloat16).astype(np.float32)
    return cosine, sine


def tables(size):
    half = size // 2
    c, s = dft_parts(size)
    order = np.concatenate([np.arange(0, size, 2), np.arange(1, size, 2)])
    fc, fs = c[order], s[order]
    left = np.block([[fc, fs], [-fs, fc]])
    cols = []
    for q in range(2):
        pick = order[q * half : (q + 1) * half]
        cols.append(np.block([[c[:, pick], -s[:, pick]], [s[:, pick], c[:, pick]]]))
    right = np.concatenate(cols, 1)
    gl, gr = [], []
    for q in range(2):
        ce, se = c[:half, q::2], s[:half, q::2]
        gl.append(np.block([[ce, -se], [se, ce]]))
        cr, sr = c[q::2, :half], s[q::2, :half]
        gr.append(np.block([[cr, sr], [-sr, cr]]))
    perm = np.zeros((size, size), np.float32)
    perm[np.arange(size), order] = 1.0
    to = lambda a: jnp.asarray(np.asarray(a, np.float32).astype(jnp.bfloat16))
    return to(left), to(right), to(np.stack(gl)), to(np.stack(gr)), to(perm), to(perm.T)


def prep_kernel(frames, rows, cols, out):
    def one(s, _):
        a = jnp.dot(rows[...], frames[s], preferred_element_type=f32).astype(bf16)
        out[s] = jnp.dot(a, cols[...], preferred_element_type=f32).astype(bf16)
        return 0

    lax.fori_loop(0, frames.shape[0], one, 0)


def choose(pos, cnt, wanted, todo, frames_hbm, frames, sem):
    todo[0] = 0

    def pick(s, k):
        take = wanted(pos[s, 1])

        @pl.when(take)
        def _():
            todo[k] = s
            pltpu.make_async_copy(frames_hbm.at[s], frames.at[s], sem.at[s]).start()

        return k + take.astype(jnp.int32)

    return lax.fori_loop(0, cnt[0], pick, 0)


def await_frames(count, todo, frames_hbm, frames, sem):
    def one(k, _):
        s = todo[k]
        pltpu.make_async_copy(frames_hbm.at[s], frames.at[s], sem.at[s]).wait()
        return 0

    lax.fori_loop(0, count, one, 0)


def positions_pass(
    pos, count, base, blocks, clear, probe, frames, tables, p_out,
    ext, gext, pat, xs, hs, sp, ws, ib, hb, eb, todo,
):
    left, right, gl, gr = tables
    n = probe.shape[-1]
    h = n // 2
    ch = 16
    last = jnp.maximum(count - 1, 0)

    def window(t):
        s = todo[jnp.clip(t, 0, last)]
        c = pos[s, 1]
        sh = lax.rem(c, 128)
        cb = jnp.clip(c // 128 - base, 0, blocks - 3)
        return s, pos[s, 0], cb, sh, lax.rem(384 - sh, 384)

    def patch_rows(win, i, ch=16):
        _, r, cb, _, unshift = win
        out = []
        for p in range(2):
            w = jnp.concatenate([ext[p, cb + b, pl.ds(r + i, ch), :] for b in range(3)], 1)
            out.append(pltpu.roll(w, unshift, 1)[:, :n])
        return out

    def wave_rows(win, slot, i):
        o = patch_rows(win, i)
        for p in range(2):
            pat[slot, p, i : i + ch, :] = o[p]
        for m in range(2):
            pr = probe[m, 0, i : i + ch, :]
            pi = probe[m, 1, i : i + ch, :]
            xs[m, i : i + ch, :] = (pr * o[0] - pi * o[1]).astype(bf16)
            xs[m, n + i : n + i + ch, :] = (pr * o[1] + pi * o[0]).astype(bf16)

    def forward_left(m, part):
        half = jnp.dot(left[part * n : (part + 1) * n, :], xs[m], preferred_element_type=f32)
        hs[m, :, part * n : (part + 1) * n] = half.astype(bf16)

    def forward_right(m, q):
        sp[m, q] = jnp.dot(hs[m], right[:, q * n : (q + 1) * n], preferred_element_type=f32)

    def weigh_rows(win, q, i):
        s = win[0]
        rows = i % h
        par = i // h
        v = [sp[m, q, i : i + ch, :] for m in range(2)]
        e = v[0] * v[0] + v[1] * v[1]
        inten = e[:, :h] + e[:, h:] + 1.0
        f = 1.0 - frames[s, i : i + ch, q * h : (q + 1) * h].astype(f32) * lax.rsqrt(inten)
        for m in range(2):
            for part in range(2):
                ws[m, par, part * h + rows : part * h + rows + ch, q * h : (q + 1) * h] = (
                    v[m][:, part * h : (part + 1) * h] * f
                ).astype(bf16)

    def inverse_left(m, par):
        ib[m, par] = jnp.dot(gl[par], ws[m, par], preferred_element_type=f32)

    def join_rows(m, part, i):
        a = ib[m, 0, part * h + i : part * h + i + ch, :]
        b = ib[m, 1, part * h + i : part * h + i + ch, :]
        up = (a + b).astype(bf16)
        dn = (a - b).astype(bf16)
        for q in range(2):
            hb[m, q, i : i + ch, part * h : (part + 1) * h] = up[:, q * h : (q + 1) * h]
            hb[m, q, h + i : h + i + ch, part * h : (part + 1) * h] = dn[:, q * h : (q + 1) * h]

    def inverse_right(m, q):
        eb[m, q] = jnp.dot(hb[m, q], gr[q], preferred_element_type=f32)

    def add_rows(win, slot, i0):
        for i in range(i0, i0 + ch, 8):
            add_some(win, slot, i)

    def add_some(win, slot, i):
        _, r, cb, sh, _ = win
        ore = pat[slot, 0, i : i + 8, :]
        oim = pat[slot, 1, i : i + 8, :]
        acc = None
        for m in range(2):
            e = eb[m, 0, i : i + 8, :]
            d = eb[m, 1, i : i + 8, :]
            up = e + d
            dn = e - d
            bre = jnp.concatenate([up[:, :h], dn[:, :h]], 1)
            bim = jnp.concatenate([up[:, h:], dn[:, h:]], 1)
            pr = probe[m, 0, i : i + 8, :]
            pi = probe[m, 1, i : i + 8, :]
            g = (pr * bre + pi * bim, pr * bim - pi * bre)
            acc = g if m == 0 else (acc[0] + g[0], acc[1] + g[1])
            p_out[m, 0, i : i + 8, :] += ore * bre + oim * bim
            p_out[m, 1, i : i + 8, :] += ore * bim - oim * bre
        zero = jnp.zeros((8, 128), f32)
        v = [pltpu.roll(jnp.concatenate([x, zero], 1), sh, 1) for x in acc]
        new = [
            gext[p, cb + b, pl.ds(r + i, 8), :] + v[p][:, b * 128 : (b + 1) * 128]
            for p in range(2)
            for b in range(3)
        ]
        for p in range(2):
            for b in range(3):
                gext[p, cb + b, pl.ds(r + i, 8), :] = new[p * 3 + b]

    chunks = list(range(0, n, ch))
    pairs = [(m, k) for m in range(2) for k in range(2)]

    def front(t):
        now = window(t)
        slot = lax.rem(t, 2)
        for i in chunks:
            wave_rows(now, slot, i)
        for m, part in pairs:
            forward_left(m, part)
        for q in range(2):
            for m in range(2):
                forward_right(m, q)
            for i in chunks:
                weigh_rows(now, q, i)

    def rear(t):
        old = window(t)
        slot = lax.rem(t, 2)
        for m in range(2):
            for par in range(2):
                inverse_left(m, par)
            for part in range(2):
                for i in range(0, h, ch):
                    join_rows(m, part, i)
            for q in range(2):
                inverse_right(m, q)
        for i in chunks:
            add_rows(old, slot, i)

    def both(t, _):
        now = window(t)
        old = window(t - 1)
        new_slot = lax.rem(t, 2)
        old_slot = 1 - new_slot
        for k, (m, par) in enumerate(pairs):
            inverse_left(m, par)
            for i in chunks[2 * k : 2 * k + 2]:
                wave_rows(now, new_slot, i)
        for m in range(2):
            for part in range(2):
                for i in range(0, h, ch):
                    join_rows(m, part, i)
        for k, (m, q) in enumerate(pairs):
            inverse_right(m, q)
            for i in chunks[8 + 2 * k : 8 + 2 * k + 2]:
                wave_rows(now, new_slot, i)
        for k, (m, part) in enumerate(pairs):
            forward_left(m, part)
            for i in chunks[3 * k : 3 * k + 3]:
                add_rows(old, old_slot, i)
        for m in range(2):
            forward_right(m, 0)
            for i in chunks[12 + 2 * m : 12 + 2 * m + 2]:
                add_rows(old, old_slot, i)
        for m in range(2):
            forward_right(m, 1)
            for i in chunks[8 * m : 8 * m + 8]:
                weigh_rows(now, 0, i)
        for i in chunks:
            weigh_rows(now, 1, i)
        return 0

    @pl.when(count > 0)
    def _():
        front(0)

    clear()
    lax.fori_loop(1, count, both, 0)

    @pl.when(count > 0)
    def _():
        rear(count - 1)


def fill(ext, sources):
    for p in range(2):
        for src, c_from, c_to, r0, c0 in sources:
            for b in range((c_to - c_from) // 128):
                lo = c_from + b * 128
                ext[p, c0 // 128 + b, r0 : r0 + src.shape[1], :] = src[p, :, lo : lo + 128].astype(f32)


def drain(gext, targets):
    for p in range(2):
        for dst, d0, width, r0, c0 in targets:
            for b in range(width // 128):
                dst[p, :, d0 + b * 128 : d0 + (b + 1) * 128] = gext[
                    p, c0 // 128 + b, r0 : r0 + dst.shape[1], :
                ].astype(dst.dtype)


def fetch(sources, targets, sems):
    copies = [pltpu.make_async_copy(s, d, sems.at[k]) for k, (s, d) in enumerate(zip(sources, targets))]
    for copy in copies:
        copy.start()
    return copies


def send_out(source, target, sem):
    copy = pltpu.make_async_copy(source, target, sem)
    copy.start()
    return copy


def inner_kernel(
    pos, cnt, own_hbm, below_hbm, probe_hbm, frames_hbm, left_hbm, right_hbm, gl_hbm, gr_hbm,
    g_own_hbm, g_below_hbm, carry_hbm, p_hbm,
    own, below, probe, frames, left, right, gl, gr, sems, frame_sems, out_sems, g_own, g_below, p_out,
    ext, gext, *scratch,
):
    copies = fetch(
        (own_hbm, below_hbm, probe_hbm, left_hbm, right_hbm, gl_hbm, gr_hbm),
        (own, below, probe, left, right, gl, gr),
        sems,
    )
    n = probe.shape[-1]
    tr, tc = own.shape[1:]
    inner = tc - n
    todo = scratch[-1]
    count = choose(pos, cnt, lambda c: c < inner, todo, frames_hbm, frames, frame_sems)
    copies[0].wait()
    fill(ext, ((own, 0, tc, 0, 0),))
    copies[1].wait()
    fill(ext, ((below, 0, tc, tr, 0),))
    for copy in copies[2:]:
        copy.wait()
    await_frames(count, todo, frames_hbm, frames, frame_sems)

    def clear():
        gext[...] = jnp.zeros_like(gext)
        p_out[...] = jnp.zeros_like(p_out)

    positions_pass(
        pos, count, 0, tc // 128, clear, probe, frames, (left, right, gl, gr), p_out,
        ext, gext, *scratch,
    )
    done = [send_out(p_out, p_hbm, out_sems.at[0])]
    for p in range(2):
        done.append(send_out(gext.at[p, pl.ds(inner // 128, n // 128)], carry_hbm.at[p], out_sems.at[1 + p]))
    drain(gext, ((g_below, 0, inner, tr, 0),))
    done.append(send_out(g_below, g_below_hbm, out_sems.at[3]))
    drain(gext, ((g_own, 0, inner, 0, 0),))
    done.append(send_out(g_own, g_own_hbm, out_sems.at[4]))
    for copy in done:
        copy.wait()


def edge_kernel(
    scale, pos, cnt, core, own_hbm, below_hbm, strip_hbm, corner_hbm, carry_hbm, p_hbm, band_hbm, probe_hbm, frames_hbm,
    left_hbm, right_hbm, gl_hbm, gr_hbm,
    g_own_hbm, g_rows_hbm, g_strip_hbm, p_keep_hbm, p_send_hbm,
    own, below, strip, corner, carry, p_in, probe, frames, left, right, gl, gr, sems, frame_sems, out_sems,
    g_own, g_rows, g_strip, p_keep, p_send, p_out, ext, gext, *scratch,
):
    n = probe.shape[-1]
    tr, tc = own_hbm.shape[1:]
    inner = tc - n
    copies = fetch(
        (
            own_hbm.at[:, :, inner:tc], below_hbm.at[:, :, inner:tc], strip_hbm, corner_hbm, probe_hbm,
            left_hbm, right_hbm, gl_hbm, gr_hbm, p_hbm, carry_hbm, band_hbm,
        ),
        (own, below, strip, corner, probe, left, right, gl, gr, p_in, carry, g_rows.at[:, :, pl.ds(0, inner)]),
        sems,
    )
    todo = scratch[-1]
    count = choose(pos, cnt, lambda c: c >= inner, todo, frames_hbm, frames, frame_sems)
    for copy in copies[:4]:
        copy.wait()
    fill(ext, ((own, 0, n, 0, 0), (below, 0, n, tr, 0), (strip, 0, n, 0, n), (corner, 0, n, tr, n)))
    for copy in copies[4:9]:
        copy.wait()
    await_frames(count, todo, frames_hbm, frames, frame_sems)

    def clear():
        for copy in copies[9:]:
            copy.wait()
        p_out[...] = p_in[...]
        for p in range(2):
            for b in range(n // 128):
                gext[p, b] = carry[p, b]
                gext[p, n // 128 + b] = jnp.zeros_like(gext[p, b])

    positions_pass(
        pos, count, inner // 128, 2 * n // 128, clear, probe, frames,
        (left, right, gl, gr), p_out, ext, gext, *scratch,
    )
    p_send[...] = (p_out[1 - core[0]] * scale).astype(bf16)
    done = [send_out(p_send, p_send_hbm, out_sems.at[0])]
    p_keep[...] = p_out[core[0]] * scale
    done.append(send_out(p_keep, p_keep_hbm, out_sems.at[1]))
    drain(gext, ((g_rows, inner, 2 * n, tr, 0),))
    done.append(send_out(g_rows, g_rows_hbm, out_sems.at[2]))
    drain(gext, ((g_strip, 0, n, 0, n),))
    done.append(send_out(g_strip, g_strip_hbm, out_sems.at[3]))
    drain(gext, ((g_own, 0, n, 0, 0),))
    done.append(send_out(g_own, g_own_hbm, out_sems.at[4]))
    for copy in done:
        copy.wait()


def body(object_field, probe, measured, positions, counts):
    size = probe.shape[-1]
    tile_rows, tile_cols = object_field.shape[1:]
    slots = measured.shape[2]
    left, right, gl, gr, perm, perm_t = tables(size)
    vmem = pl.BlockSpec(memory_space=pltpu.VMEM)
    stay = pl.BlockSpec(memory_space=pl.ANY)
    smem = pl.BlockSpec(memory_space=pltpu.SMEM)
    pos, cnt = positions[0, 0], counts[0]
    core = (lax.axis_index("row") & 1).astype(jnp.int32).reshape(1)
    inner = tile_cols - size
    rows, cols = tile_rows + size, tile_cols + size

    below = shifted(object_field, "row", -1)
    strip = shifted(object_field[:, :, :size], "col", -1)
    corner = shifted(strip, "row", -1)
    frames = pl.pallas_call(
        prep_kernel,
        out_shape=jax.ShapeDtypeStruct(measured.shape[2:], bf16),
        in_specs=[vmem] * 3,
        out_specs=vmem,
        compiler_params=pltpu.CompilerParams(vmem_limit_bytes=8 * 2**20),
        cost_estimate=pl.CostEstimate(
            flops=slots * 4 * size**3, bytes_accessed=4 * slots * size * size, transcendentals=0
        ),
    )(measured[0, 0], perm, perm_t)

    def scratch(blocks):
        return [
            pltpu.VMEM((2, blocks, rows, 128), f32),
            pltpu.VMEM((2, blocks, rows, 128), f32),
            pltpu.VMEM((2, 2, size, size), f32),
            pltpu.VMEM((2, 2 * size, size), bf16),
            pltpu.VMEM((2, size, 2 * size), bf16),
            pltpu.VMEM((2, 2, size, size), f32),
            pltpu.VMEM((2, 2, size, size), bf16),
            pltpu.VMEM((2, 2, size, size), f32),
            pltpu.VMEM((2, 2, size, size), bf16),
            pltpu.VMEM((2, 2, size, size), f32),
            pltpu.SMEM((slots,), jnp.int32),
        ]

    fixed = [pltpu.VMEM(x.shape, x.dtype) for x in (probe, frames, left, right, gl, gr)]
    params = pltpu.CompilerParams(
        vmem_limit_bytes=60 * 2**20
    )
    g_main, g_band, carry, p_part = pl.pallas_call(
        inner_kernel,
        out_shape=(
            jax.ShapeDtypeStruct((2, tile_rows, inner), f32),
            jax.ShapeDtypeStruct((2, size, inner), bf16),
            jax.ShapeDtypeStruct((2, size // 128, rows, 128), f32),
            jax.ShapeDtypeStruct(probe.shape, f32),
        ),
        in_specs=[smem, smem] + [stay] * 8,
        out_specs=[stay] * 4,
        scratch_shapes=[
            pltpu.VMEM((2, tile_rows, tile_cols), bf16),
            pltpu.VMEM((2, size, tile_cols), bf16),
        ]
        + fixed
        + [pltpu.SemaphoreType.DMA((k,)) for k in (7, slots, 5)]
        + [
            pltpu.VMEM((2, tile_rows, inner), f32),
            pltpu.VMEM((2, size, inner), bf16),
            pltpu.VMEM(probe.shape, f32),
        ]
        + scratch(tile_cols // 128),
        compiler_params=params,
        cost_estimate=pl.CostEstimate(flops=9 * 2**30, bytes_accessed=12 * 2**20, transcendentals=0),
    )(pos, cnt, object_field, below, probe, frames, left, right, gl, gr)
    total = slots * lax.axis_size("row") * lax.axis_size("col")
    scale = 1.0 / math.sqrt(total)
    g_right, g_rows, g_strip, p_keep, p_send = pl.pallas_call(
        lambda *refs: edge_kernel(scale, *refs),
        out_shape=(
            jax.ShapeDtypeStruct((2, tile_rows, size), f32),
            jax.ShapeDtypeStruct((2, size, cols), bf16),
            jax.ShapeDtypeStruct((2, tile_rows, size), bf16),
            jax.ShapeDtypeStruct(probe.shape[1:], f32),
            jax.ShapeDtypeStruct(probe.shape[1:], bf16),
        ),
        in_specs=[smem] * 3 + [stay] * 13,
        out_specs=[stay] * 5,
        scratch_shapes=[
            pltpu.VMEM((2, tile_rows, size), bf16),
            pltpu.VMEM((2, size, size), bf16),
            pltpu.VMEM((2, tile_rows, size), bf16),
            pltpu.VMEM((2, size, size), bf16),
            pltpu.VMEM((2, size // 128, rows, 128), f32),
            pltpu.VMEM(probe.shape, f32),
        ]
        + fixed
        + [pltpu.SemaphoreType.DMA((k,)) for k in (12, slots, 5)]
        + [
            pltpu.VMEM((2, tile_rows, size), f32),
            pltpu.VMEM((2, size, cols), bf16),
            pltpu.VMEM((2, tile_rows, size), bf16),
            pltpu.VMEM(probe.shape[1:], f32),
            pltpu.VMEM(probe.shape[1:], bf16),
            pltpu.VMEM(probe.shape, f32),
        ]
        + scratch(2 * size // 128),
        compiler_params=params,
        cost_estimate=pl.CostEstimate(flops=3 * 2**30, bytes_accessed=12 * 2**20, transcendentals=0),
    )(pos, cnt, core, object_field, below, strip, corner, carry, p_part, g_band, probe, frames, left, right, gl, gr)

    tail = shifted(g_rows, "row", 1)
    to_right = (g_strip.astype(f32) + tail[:, :, tile_cols:].astype(f32)).astype(bf16)
    side = shifted(to_right, "col", 1)
    probe_grad = reduce_all(p_keep.reshape(-1, size), p_send.reshape(-1, size)).reshape(probe.shape)
    object_grad = jnp.concatenate([g_main, g_right], 2) + tail[:, :, :tile_cols].astype(f32)
    object_grad = object_grad.at[:, :, :size].add(side.astype(f32))
    return (object_grad, probe_grad)


def solution(mesh):
    placed = (
        P(None, "row", "col"),
        P(),
        P("row", "col", None, None, None),
        P("row", "col", None, None),
        P("row", "col"),
    )
    return jax.shard_map(body, mesh=mesh, in_specs=placed, out_specs=(P(None, "row", "col"), P()), check_vma=False)
```

```python
import math

import jax
import jax.numpy as jnp
import numpy as np
from jax import lax
from jax.experimental import pallas as pl
from jax.experimental.pallas import tpu as pltpu
from jax.sharding import PartitionSpec as P


f32 = jnp.float32
bf16 = jnp.bfloat16


def shifted(x, axis, by):
    peers = lax.axis_size(axis)
    pairs = [(i, i + by) for i in range(peers) if 0 <= i + by < peers]
    return lax.ppermute(x, axis, pairs)


Y = [(8, 0), (16, 0), (24, 0)]
X = [(0, 2), (0, 4), (0, 6)]
FIELDS = {
    "core": ([(1, 0)], [(1, 0)]),
    "first": (Y, X),
    "second": (X, Y),
    "z0": ([(2, 0)], [(2, 0)]),
    "z1": ([(4, 0)], [(4, 0)]),
    "z2": ([(4, 1)], [(4, 1)]),
}


def partner(v, field, d):
    masks = [masks[d - 1] for masks in FIELDS[field]]
    rows, cols = lax.axis_size("row"), lax.axis_size("col")
    pairs = []
    for r in range(rows):
        for c in range(cols):
            row, col = masks[r & 1]
            pairs.append((r * cols + c, (r ^ row) * cols + (c ^ col)))
    return lax.ppermute(v, ("row", "col"), pairs)


def members(field):
    return len(FIELDS[field][0]) + 1


def place(field):
    if field == "core":
        return lax.axis_index("row") & 1
    return jnp.where(lax.axis_index("row") & 1 == 0, lax.axis_index("row") >> 3, lax.axis_index("col") >> 1)


def scatter_sum(v, field, dtype):
    n = members(field)
    g = place(field)
    k = v.shape[0] // n
    total = lax.dynamic_slice_in_dim(v, g * k, k, 0)
    got = [
        partner(lax.dynamic_slice_in_dim(v, (g ^ d) * k, k, 0).astype(dtype), field, d)
        for d in range(1, n)
    ]
    for part in got:
        total = total + part.astype(f32)
    return total


def full_sum(v, field, dtype):
    n = members(field)
    sent = v.astype(dtype)
    parts = [sent.astype(f32)] + [partner(sent, field, d).astype(f32) for d in range(1, n)]
    while len(parts) > 1:
        parts = [parts[i] + parts[i + 1] for i in range(0, len(parts), 2)]
    return parts[0]


def gather(v, field, dtype):
    n = members(field)
    g = place(field)
    k = v.shape[0]
    sent = v.astype(dtype)
    got = [partner(sent, field, d) for d in range(1, n)]
    out = jnp.zeros((n * k,) + v.shape[1:], dtype)
    out = lax.dynamic_update_slice_in_dim(out, sent, g * k, 0)
    for d in range(1, n):
        out = lax.dynamic_update_slice_in_dim(out, got[d - 1], (g ^ d) * k, 0)
    return out


PLAN = (
    (scatter_sum, "first", bf16),
    (full_sum, "z0", bf16),
    (full_sum, "z1", bf16),
    (full_sum, "z2", bf16),
    (full_sum, "second", bf16),
    (gather, "first", bf16),
    (gather, "core", bf16),
)


def reduce_all(keep, send):
    v = keep + partner(send, "core", 1).astype(f32)
    for step, field, dtype in PLAN:
        v = step(v, field, dtype)
    return v.astype(f32)


def dft_parts(size):
    index = np.arange(size)
    phase = (index[:, None] * index[None, :]) % size
    angle = 2.0 * np.pi / size * phase
    cosine = (np.cos(angle) / np.sqrt(size)).astype(jnp.bfloat16).astype(np.float32)
    sine = (np.sin(angle) / np.sqrt(size)).astype(jnp.bfloat16).astype(np.float32)
    return cosine, sine


def tables(size):
    half = size // 2
    c, s = dft_parts(size)
    order = np.concatenate([np.arange(0, size, 2), np.arange(1, size, 2)])
    fc, fs = c[order], s[order]
    left = np.block([[fc, fs], [-fs, fc]])
    cols = []
    for q in range(2):
        pick = order[q * half : (q + 1) * half]
        cols.append(np.block([[c[:, pick], -s[:, pick]], [s[:, pick], c[:, pick]]]))
    right = np.concatenate(cols, 1)
    gl, gr = [], []
    for q in range(2):
        ce, se = c[:half, q::2], s[:half, q::2]
        gl.append(np.block([[ce, -se], [se, ce]]))
        cr, sr = c[q::2, :half], s[q::2, :half]
        gr.append(np.block([[cr, sr], [-sr, cr]]))
    perm = np.zeros((size, size), np.float32)
    perm[np.arange(size), order] = 1.0
    to = lambda a: jnp.asarray(np.asarray(a, np.float32).astype(jnp.bfloat16))
    return to(left), to(right), to(np.stack(gl)), to(np.stack(gr)), to(perm), to(perm.T)


def prep_kernel(frames, rows, cols, out):
    def one(s, _):
        a = jnp.dot(rows[...], frames[s], preferred_element_type=f32).astype(bf16)
        out[s] = jnp.dot(a, cols[...], preferred_element_type=f32).astype(bf16)
        return 0

    lax.fori_loop(0, frames.shape[0], one, 0)


def choose(pos, cnt, wanted, todo, frames_hbm, frames, sem):
    todo[0] = 0

    def pick(s, k):
        take = wanted(pos[s, 1])

        @pl.when(take)
        def _():
            todo[k] = s
            pltpu.make_async_copy(frames_hbm.at[s], frames.at[s], sem.at[s]).start()

        return k + take.astype(jnp.int32)

    return lax.fori_loop(0, cnt[0], pick, 0)


def await_frames(count, todo, frames_hbm, frames, sem):
    def one(k, _):
        s = todo[k]
        pltpu.make_async_copy(frames_hbm.at[s], frames.at[s], sem.at[s]).wait()
        return 0

    lax.fori_loop(0, count, one, 0)


def positions_pass(
    pos, count, base, blocks, clear, probe, frames, tables, p_out,
    ext, gext, pat, xs, hs, sp, ws, ib, hb, eb, todo,
):
    left, right, gl, gr = tables
    n = probe.shape[-1]
    h = n // 2
    ch = 16
    last = jnp.maximum(count - 1, 0)

    def window(t):
        s = todo[jnp.clip(t, 0, last)]
        c = pos[s, 1]
        sh = lax.rem(c, 128)
        cb = jnp.clip(c // 128 - base, 0, blocks - 3)
        return s, pos[s, 0], cb, sh, lax.rem(384 - sh, 384)

    def patch_rows(win, i, ch=16):
        _, r, cb, _, unshift = win
        out = []
        for p in range(2):
            w = jnp.concatenate([ext[p, cb + b, pl.ds(r + i, ch), :] for b in range(3)], 1)
            out.append(pltpu.roll(w, unshift, 1)[:, :n])
        return out

    def wave_rows(win, slot, i):
        o = patch_rows(win, i)
        for p in range(2):
            pat[slot, p, i : i + ch, :] = o[p]
        for m in range(2):
            pr = probe[m, 0, i : i + ch, :]
            pi = probe[m, 1, i : i + ch, :]
            xs[m, i : i + ch, :] = (pr * o[0] - pi * o[1]).astype(bf16)
            xs[m, n + i : n + i + ch, :] = (pr * o[1] + pi * o[0]).astype(bf16)

    def forward_left(m, part):
        half = jnp.dot(left[part * n : (part + 1) * n, :], xs[m], preferred_element_type=f32)
        hs[m, :, part * n : (part + 1) * n] = half.astype(bf16)

    def forward_right(m, q):
        sp[m, q] = jnp.dot(hs[m], right[:, q * n : (q + 1) * n], preferred_element_type=f32)

    def weigh_rows(win, q, i):
        s = win[0]
        rows = i % h
        par = i // h
        v = [sp[m, q, i : i + ch, :] for m in range(2)]
        e = v[0] * v[0] + v[1] * v[1]
        inten = e[:, :h] + e[:, h:] + 1.0
        f = 1.0 - frames[s, i : i + ch, q * h : (q + 1) * h].astype(f32) * lax.rsqrt(inten)
        for m in range(2):
            for part in range(2):
                ws[m, par, part * h + rows : part * h + rows + ch, q * h : (q + 1) * h] = (
                    v[m][:, part * h : (part + 1) * h] * f
                ).astype(bf16)

    def inverse_left(m, par):
        ib[m, par] = jnp.dot(gl[par], ws[m, par], preferred_element_type=f32)

    def join_rows(m, part, i):
        a = ib[m, 0, part * h + i : part * h + i + ch, :]
        b = ib[m, 1, part * h + i : part * h + i + ch, :]
        up = (a + b).astype(bf16)
        dn = (a - b).astype(bf16)
        for q in range(2):
            hb[m, q, i : i + ch, part * h : (part + 1) * h] = up[:, q * h : (q + 1) * h]
            hb[m, q, h + i : h + i + ch, part * h : (part + 1) * h] = dn[:, q * h : (q + 1) * h]

    def inverse_right(m, q):
        eb[m, q] = jnp.dot(hb[m, q], gr[q], preferred_element_type=f32)

    def add_rows(win, slot, i0):
        for i in range(i0, i0 + ch, 8):
            add_some(win, slot, i)

    def add_some(win, slot, i):
        _, r, cb, sh, _ = win
        ore = pat[slot, 0, i : i + 8, :]
        oim = pat[slot, 1, i : i + 8, :]
        acc = None
        for m in range(2):
            e = eb[m, 0, i : i + 8, :]
            d = eb[m, 1, i : i + 8, :]
            up = e + d
            dn = e - d
            bre = jnp.concatenate([up[:, :h], dn[:, :h]], 1)
            bim = jnp.concatenate([up[:, h:], dn[:, h:]], 1)
            pr = probe[m, 0, i : i + 8, :]
            pi = probe[m, 1, i : i + 8, :]
            g = (pr * bre + pi * bim, pr * bim - pi * bre)
            acc = g if m == 0 else (acc[0] + g[0], acc[1] + g[1])
            p_out[m, 0, i : i + 8, :] += ore * bre + oim * bim
            p_out[m, 1, i : i + 8, :] += ore * bim - oim * bre
        zero = jnp.zeros((8, 128), f32)
        v = [pltpu.roll(jnp.concatenate([x, zero], 1), sh, 1) for x in acc]
        new = [
            gext[p, cb + b, pl.ds(r + i, 8), :] + v[p][:, b * 128 : (b + 1) * 128]
            for p in range(2)
            for b in range(3)
        ]
        for p in range(2):
            for b in range(3):
                gext[p, cb + b, pl.ds(r + i, 8), :] = new[p * 3 + b]

    chunks = list(range(0, n, ch))
    pairs = [(m, k) for m in range(2) for k in range(2)]

    def front(t):
        now = window(t)
        slot = lax.rem(t, 2)
        for i in chunks:
            wave_rows(now, slot, i)
        for m, part in pairs:
            forward_left(m, part)
        for q in range(2):
            for m in range(2):
                forward_right(m, q)
            for i in chunks:
                weigh_rows(now, q, i)

    def rear(t):
        old = window(t)
        slot = lax.rem(t, 2)
        for m in range(2):
            for par in range(2):
                inverse_left(m, par)
            for part in range(2):
                for i in range(0, h, ch):
                    join_rows(m, part, i)
            for q in range(2):
                inverse_right(m, q)
        for i in chunks:
            add_rows(old, slot, i)

    def both(t, _):
        now = window(t)
        old = window(t - 1)
        new_slot = lax.rem(t, 2)
        old_slot = 1 - new_slot
        for k, (m, par) in enumerate(pairs):
            inverse_left(m, par)
            for i in chunks[2 * k : 2 * k + 2]:
                wave_rows(now, new_slot, i)
        for m in range(2):
            for part in range(2):
                for i in range(0, h, ch):
                    join_rows(m, part, i)
        for k, (m, q) in enumerate(pairs):
            inverse_right(m, q)
            for i in chunks[8 + 2 * k : 8 + 2 * k + 2]:
                wave_rows(now, new_slot, i)
        for k, (m, part) in enumerate(pairs):
            forward_left(m, part)
            for i in chunks[3 * k : 3 * k + 3]:
                add_rows(old, old_slot, i)
        for m in range(2):
            forward_right(m, 0)
            for i in chunks[12 + 2 * m : 12 + 2 * m + 2]:
                add_rows(old, old_slot, i)
        for m in range(2):
            forward_right(m, 1)
            for i in chunks[8 * m : 8 * m + 8]:
                weigh_rows(now, 0, i)
        for i in chunks:
            weigh_rows(now, 1, i)
        return 0

    @pl.when(count > 0)
    def _():
        front(0)

    clear()
    lax.fori_loop(1, count, both, 0)

    @pl.when(count > 0)
    def _():
        rear(count - 1)


def fill(ext, sources):
    for p in range(2):
        for src, c_from, c_to, r0, c0 in sources:
            for b in range((c_to - c_from) // 128):
                lo = c_from + b * 128
                ext[p, c0 // 128 + b, r0 : r0 + src.shape[1], :] = src[p, :, lo : lo + 128].astype(f32)


def drain(gext, targets):
    for p in range(2):
        for dst, d0, width, r0, c0 in targets:
            for b in range(width // 128):
                dst[p, :, d0 + b * 128 : d0 + (b + 1) * 128] = gext[
                    p, c0 // 128 + b, r0 : r0 + dst.shape[1], :
                ].astype(dst.dtype)


def fetch(sources, targets, sems):
    copies = [pltpu.make_async_copy(s, d, sems.at[k]) for k, (s, d) in enumerate(zip(sources, targets))]
    for copy in copies:
        copy.start()
    return copies


def send_out(source, target, sem):
    copy = pltpu.make_async_copy(source, target, sem)
    copy.start()
    return copy


def tile_kernel(
    scale, pos, cnt, core, own_hbm, below_hbm, strip_hbm, corner_hbm, probe_hbm, frames_hbm,
    left_hbm, right_hbm, gl_hbm, gr_hbm,
    g_own_hbm, g_rows_hbm, g_strip_hbm, p_keep_hbm, p_send_hbm,
    own, below, strip, corner, probe, frames, left, right, gl, gr, sems, frame_sems, out_sems,
    g_own, g_rows, g_strip, p_keep, p_send, p_out, ext, gext, *scratch,
):
    copies = fetch(
        (own_hbm, below_hbm, strip_hbm, corner_hbm, probe_hbm, left_hbm, right_hbm, gl_hbm, gr_hbm),
        (own, below, strip, corner, probe, left, right, gl, gr),
        sems,
    )
    n = probe.shape[-1]
    tr, tc = own.shape[1:]
    todo = scratch[-1]
    count = choose(pos, cnt, lambda c: c >= 0, todo, frames_hbm, frames, frame_sems)
    copies[0].wait()
    fill(ext, ((own, 0, tc, 0, 0),))
    for copy in copies[1:4]:
        copy.wait()
    fill(ext, ((below, 0, tc, tr, 0), (strip, 0, n, 0, tc), (corner, 0, n, tr, tc)))
    for copy in copies[4:]:
        copy.wait()
    await_frames(count, todo, frames_hbm, frames, frame_sems)

    def clear():
        gext[...] = jnp.zeros_like(gext)
        p_out[...] = jnp.zeros_like(p_out)

    positions_pass(
        pos, count, 0, (tc + n) // 128, clear, probe, frames, (left, right, gl, gr), p_out,
        ext, gext, *scratch,
    )
    p_send[...] = (p_out[1 - core[0]] * scale).astype(bf16)
    done = [send_out(p_send, p_send_hbm, out_sems.at[0])]
    p_keep[...] = p_out[core[0]] * scale
    done.append(send_out(p_keep, p_keep_hbm, out_sems.at[1]))
    drain(gext, ((g_rows, 0, tc + n, tr, 0),))
    done.append(send_out(g_rows, g_rows_hbm, out_sems.at[2]))
    drain(gext, ((g_strip, 0, n, 0, tc),))
    done.append(send_out(g_strip, g_strip_hbm, out_sems.at[3]))
    drain(gext, ((g_own, 0, tc, 0, 0),))
    done.append(send_out(g_own, g_own_hbm, out_sems.at[4]))
    for copy in done:
        copy.wait()


def body(object_field, probe, measured, positions, counts):
    size = probe.shape[-1]
    tile_rows, tile_cols = object_field.shape[1:]
    slots = measured.shape[2]
    left, right, gl, gr, perm, perm_t = tables(size)
    vmem = pl.BlockSpec(memory_space=pltpu.VMEM)
    stay = pl.BlockSpec(memory_space=pl.ANY)
    smem = pl.BlockSpec(memory_space=pltpu.SMEM)
    pos, cnt = positions[0, 0], counts[0]
    core = (lax.axis_index("row") & 1).astype(jnp.int32).reshape(1)
    rows, cols = tile_rows + size, tile_cols + size

    below = shifted(object_field, "row", -1)
    strip = shifted(object_field[:, :, :size], "col", -1)
    corner = shifted(strip, "row", -1)
    frames = pl.pallas_call(
        prep_kernel,
        out_shape=jax.ShapeDtypeStruct(measured.shape[2:], bf16),
        in_specs=[vmem] * 3,
        out_specs=vmem,
        compiler_params=pltpu.CompilerParams(vmem_limit_bytes=8 * 2**20),
        cost_estimate=pl.CostEstimate(
            flops=slots * 4 * size**3, bytes_accessed=4 * slots * size * size, transcendentals=0
        ),
    )(measured[0, 0], perm, perm_t)

    def scratch(blocks):
        return [
            pltpu.VMEM((2, blocks, rows, 128), f32),
            pltpu.VMEM((2, blocks, rows, 128), f32),
            pltpu.VMEM((2, 2, size, size), f32),
            pltpu.VMEM((2, 2 * size, size), bf16),
            pltpu.VMEM((2, size, 2 * size), bf16),
            pltpu.VMEM((2, 2, size, size), f32),
            pltpu.VMEM((2, 2, size, size), bf16),
            pltpu.VMEM((2, 2, size, size), f32),
            pltpu.VMEM((2, 2, size, size), bf16),
            pltpu.VMEM((2, 2, size, size), f32),
            pltpu.SMEM((slots,), jnp.int32),
        ]

    fixed = [pltpu.VMEM(x.shape, x.dtype) for x in (probe, frames, left, right, gl, gr)]
    params = pltpu.CompilerParams(
        vmem_limit_bytes=60 * 2**20
    )
    total = slots * lax.axis_size("row") * lax.axis_size("col")
    scale = 1.0 / math.sqrt(total)
    g_own, g_rows, g_strip, p_keep, p_send = pl.pallas_call(
        lambda *refs: tile_kernel(scale, *refs),
        out_shape=(
            jax.ShapeDtypeStruct((2, tile_rows, tile_cols), f32),
            jax.ShapeDtypeStruct((2, size, cols), bf16),
            jax.ShapeDtypeStruct((2, tile_rows, size), bf16),
            jax.ShapeDtypeStruct(probe.shape[1:], f32),
            jax.ShapeDtypeStruct(probe.shape[1:], bf16),
        ),
        in_specs=[smem] * 3 + [stay] * 10,
        out_specs=[stay] * 5,
        scratch_shapes=[
            pltpu.VMEM((2, tile_rows, tile_cols), bf16),
            pltpu.VMEM((2, size, tile_cols), bf16),
            pltpu.VMEM((2, tile_rows, size), bf16),
            pltpu.VMEM((2, size, size), bf16),
        ]
        + fixed
        + [pltpu.SemaphoreType.DMA((k,)) for k in (9, slots, 5)]
        + [
            pltpu.VMEM((2, tile_rows, tile_cols), f32),
            pltpu.VMEM((2, size, cols), bf16),
            pltpu.VMEM((2, tile_rows, size), bf16),
            pltpu.VMEM(probe.shape[1:], f32),
            pltpu.VMEM(probe.shape[1:], bf16),
            pltpu.VMEM(probe.shape, f32),
        ]
        + scratch(cols // 128),
        compiler_params=params,
        cost_estimate=pl.CostEstimate(flops=slots * 2**30, bytes_accessed=16 * 2**20, transcendentals=0),
    )(pos, cnt, core, object_field, below, strip, corner, probe, frames, left, right, gl, gr)

    tail = shifted(g_rows, "row", 1)
    to_right = (g_strip.astype(f32) + tail[:, :, tile_cols:].astype(f32)).astype(bf16)
    side = shifted(to_right, "col", 1)
    probe_grad = reduce_all(p_keep.reshape(-1, size), p_send.reshape(-1, size)).reshape(probe.shape)
    object_grad = g_own + tail[:, :, :tile_cols].astype(f32)
    object_grad = object_grad.at[:, :, :size].add(side.astype(f32))
    return (object_grad, probe_grad)


def solution(mesh):
    placed = (
        P(None, "row", "col"),
        P(),
        P("row", "col", None, None, None),
        P("row", "col", None, None),
        P("row", "col"),
    )
    return jax.shard_map(
        body, mesh=mesh, in_specs=placed, out_specs=(P(None, "row", "col"), P()), check_vma=False
    )
```
